32 devices in a mesh: group: 2 (over x), expert: 16 (over z, y, core).
Axes of the slice: x: 2, y: 2, z: 4, core: 2. Of those that a mesh axis runs over, the one named last changes fastest.
Arguments:
- layer_input: bfloat16 [4096, 2048], P(('group', 'expert')), parts along dimension 0, may hold values from -6 to 6
- out_grad: bfloat16 [4096, 2048], P(('group', 'expert')), parts along dimension 0, may hold values from -6 to 6
- expert_ids: int32 [4096, 8], P(('group', 'expert')), parts along dimension 0, may hold values from 0 to 15, all different within a row; in each aligned block of 128 rows (0 to 127, 128 to 255, ...) at most 80 rows name the same one
- gates: float32 [4096, 8], P(('group', 'expert')), parts along dimension 0, may hold values from 0.05 to 1
- w_gate: bfloat16 [16, 2048, 512], P('expert'), may hold values from -0.125 to 0.125
- w_up: bfloat16 [16, 2048, 512], P('expert'), may hold values from -0.125 to 0.125
- w_down: bfloat16 [16, 512, 2048], P('expert'), may hold values from -0.25 to 0.25
Outputs:
- input_grad: float32 [4096, 2048], P(('group', 'expert')), parts along dimension 0
The draws below stay inside these ranges and needn't reach their ends.
There are 2 independent parts, one for each index of `group`. The reference program is written for one: setup_inputs(seed, part) draws one part's arguments, and reference() takes and returns one part's arrays. A program takes and returns all parts, laid end to end along the dimension named above; an argument that names none is the same for every part. Nothing has to cross between parts.
Inputs may be any that keep to these rules, and one draw needn't show every extreme that they name: `expert_ids`: within the rows of one device (aligned blocks of 128 tokens) no expert is named more than 80 times, a bound that some block reaches; a row names 8 different experts.
All inputs are finite; a program needn't handle non-finite values.
Results may differ from the reference program's by a relative error of at most 0.0041.
Values may be sent and summed in bfloat16 or wider, within the bound.
No kernel may reach another device: no remote copies, remote signals or barrier semaphores. Data moves between devices by JAX's collectives and lax.ppermute only.
A program may use at most 128 MiB of HBM per device.

```python
import math
import jax
import jax.numpy as jnp
import numpy as np
from jax import lax

D = 2048
F = 512
TOP = 8
TOK_DEV = 128
EXPERTS = 16
TOKENS = 2048
CAP = 80
N_EXPERT = 16


def block_scale(rng, extent, split, least, top_value):
    def one(dim, blocks):
        draws = jax.random.uniform(jax.random.fold_in(jax.random.fold_in(rng, 6), dim), (blocks,), jnp.float32, least / len(split), top_value / len(split))
        return jnp.repeat(jnp.exp(draws), extent[dim] // blocks).reshape((-1,) + (1,) * (len(extent) - dim - 1))

    factor_of = one(*split[0])
    for cut in split[1:]:
        factor_of = factor_of * one(*cut)
    return factor_of


def deal_out(rng, own, number, rows, amount, top, limit, slope):
    sequence = jax.random.permutation(rng, amount)
    heavy_load, common = load_shares(amount, rows * top, limit, slope, True), load_shares(amount, rows * top, limit, slope, False)
    places = jnp.arange(amount)

    def named(tallies, turn):
        used = int((tallies > 0).sum())
        fixed = max(1, used // 4)
        shifted = fixed + (places - fixed + turn * (used - fixed)) % max(1, amount - fixed)
        return jnp.zeros((amount,), jnp.int32).at[sequence[jnp.where(places < fixed, places, shifted)]].set(jnp.asarray(tallies, jnp.int32))

    tallies = jnp.where(number % 4 == 0, named(heavy_load, number // 4), named(common, number - number // 4 - 1))
    mixed = jax.random.permutation(jax.random.fold_in(own, 3), amount)
    donor, taker = mixed[0:amount // 2 * 2:2], mixed[1:amount // 2 * 2:2]
    room = jnp.minimum(tallies[donor] - 1, limit - tallies[taker]) // 2
    room = jnp.where((donor == sequence[0]) | (taker == sequence[0]) | (tallies[taker] == 0), 0, jnp.maximum(room, 0))
    shifted = jax.random.randint(jax.random.fold_in(own, 4), (amount // 2,), 0, 1 << 20) % (room + 1)
    tallies = tallies.at[donor].add(-shifted).at[taker].add(shifted)
    labels = jnp.searchsorted(jnp.cumsum(tallies), jnp.arange(rows * top), side="right").astype(jnp.int32)
    table = labels.reshape(top, rows).T
    table = table[jax.random.permutation(jax.random.fold_in(own, 1), rows)]
    turn = jax.random.randint(jax.random.fold_in(own, 2), (rows, 1), 0, top)
    return jnp.take_along_axis(table, (jnp.arange(top)[None, :] + turn) % top, axis=1)


def load_shares(count, total, limit, lean, full):
    loads = [(1 << 20) // math.isqrt(rank ** lean) + 1 for rank in range(1, count + 1)]
    largest = limit if full else min(limit, max(-(-total // count), total * loads[0] // sum(loads)))
    least = 1 if total - largest >= count - 1 else 0
    given, surplus = [largest] + [least] * (count - 1), total - largest - least * (count - 1)
    while surplus > 0:
        free = [i for i in range(1, count) if given[i] < largest] or [i for i in range(1, count) if given[i] < limit]
        mass, remaining = sum([loads[i] for i in free]), surplus
        for i in free:
            more = min(limit - given[i], max(1, remaining * loads[i] // mass), surplus)
            given[i] = given[i] + more
            surplus = surplus - more
    return np.array(given)


def normal_values(own_key, shape, scale, most, pieces=(), kind=jnp.bfloat16):
    factor_of = block_scale(own_key, shape, pieces, -0.22, 0.18) if pieces else 1.0
    values = jax.random.normal(own_key, shape, jnp.float32) * scale * factor_of
    return jnp.minimum(jnp.maximum(values, -most), most).astype(kind)


def setup_inputs(seed: int = 0, part: int = 0) -> dict:
    streams_of = jax.random.split(jax.random.key(seed), 8)
    part_keys = jax.random.split(jax.random.fold_in(streams_of[7], part), 8)
    layer_input = normal_values(part_keys[0], (TOKENS, D), 1.0, 6.0, ((0, 16),))
    out_grad = normal_values(part_keys[1], (TOKENS, D), 1.0, 6.0, ((0, 16),))
    expert_ids_keys = jax.random.split(jax.random.fold_in(part_keys[2], 1), TOKENS // TOK_DEV)
    expert_ids_turns = jax.random.permutation(jax.random.fold_in(part_keys[2], 3), TOKENS // TOK_DEV)
    expert_ids = jax.vmap(lambda own, number: deal_out(jax.random.fold_in(part_keys[2], 2), own, number, TOK_DEV, EXPERTS, TOP, CAP, 1))(expert_ids_keys, expert_ids_turns).reshape((TOKENS, TOP))
    gates = jnp.clip(jnp.exp(math.log(1.0) - 2.9957323 * jax.random.uniform(part_keys[3], (TOKENS, TOP), jnp.float32) ** block_scale(part_keys[3], (TOKENS, TOP), ((0, 16),), -0.2, 0.2)), 0.05, 1.0)
    w_gate = normal_values(streams_of[4], (EXPERTS, D, F), D ** -0.5, 0.125, ((0, 16),))
    w_up = normal_values(streams_of[5], (EXPERTS, D, F), D ** -0.5, 0.125, ((0, 16),))
    w_down = normal_values(streams_of[6], (EXPERTS, F, D), F ** -0.5, 0.25, ((0, 16),))
    return {"layer_input": layer_input, "out_grad": out_grad, "expert_ids": expert_ids, "gates": gates, "w_gate": w_gate, "w_up": w_up, "w_down": w_down}


def expert_rows(rows_in, rows_grad, gate_w, up_w, down_w):
    pre_gate = jnp.dot(rows_in, gate_w, preferred_element_type=jnp.float32)
    pre_up = jnp.dot(rows_in, up_w, preferred_element_type=jnp.float32)
    back = lax.dot_general(rows_grad, down_w, (((1,), (1,)), ((), ())), preferred_element_type=jnp.float32)
    sig = jax.nn.sigmoid(pre_gate)
    d_gate = (back * pre_up * sig * (1.0 + pre_gate * (1.0 - sig))).astype(jnp.bfloat16)
    d_up = (back * pre_gate * sig).astype(jnp.bfloat16)
    term = lax.dot_general(d_gate, gate_w, (((1,), (1,)), ((), ())), preferred_element_type=jnp.float32)
    term = term + lax.dot_general(d_up, up_w, (((1,), (1,)), ((), ())), preferred_element_type=jnp.float32)
    return term


def reference(layer_input, out_grad, expert_ids, gates, w_gate, w_up, w_down):
    flat_ids = expert_ids.reshape(-1)
    flat_gates = gates.reshape(-1)
    slots = N_EXPERT * CAP

    def one_expert(total, index):
        mask = flat_ids == index
        keys = jnp.where(mask, 0, 1).astype(jnp.int32)
        order = jnp.argsort(keys, stable=True)[:slots].astype(jnp.int32)
        valid = mask[order]
        token = order // TOP
        rows_in = jnp.where(valid[:, None], layer_input[token], jnp.zeros((), jnp.bfloat16))
        gate_val = jnp.where(valid, flat_gates[order], jnp.float32(0.0))
        rows_grad = (gate_val[:, None] * out_grad[token].astype(jnp.float32)).astype(jnp.bfloat16)
        term = expert_rows(rows_in, rows_grad, w_gate[index], w_up[index], w_down[index])
        term = jnp.where(valid[:, None], term, jnp.float32(0.0))
        return total.at[token].add(term), None

    start = jnp.zeros((TOKENS, D), jnp.float32)
    total, unused = lax.scan(one_expert, start, jnp.arange(EXPERTS, dtype=jnp.int32))
    return total
```

```python
from functools import partial

import jax
import jax.numpy as jnp
from jax import lax
from jax.experimental import pallas as pl
from jax.experimental.pallas import tpu as pltpu
from jax.sharding import PartitionSpec as P

F32 = jnp.float32
BF16 = jnp.bfloat16
LAST = (((1,), (1,)), ((), ()))


def pair_kernel(blocks, first, wide, order, *refs):
    xs, gs = refs[:blocks], refs[blocks : 2 * blocks]
    gates = refs[2 * blocks]
    weights = refs[2 * blocks + 1 : 2 * blocks + 7]
    outs = refs[2 * blocks + 7 : 3 * blocks + 7]
    x_buf, g_buf, w_in, w_out, d_buf, sems = refs[3 * blocks + 7 :]
    rows = xs[0].shape[0]
    width, hidden = weights[0].shape
    copies = {}

    def start(key, source, target):
        copies[key] = pltpu.make_async_copy(source, target, sems.at[len(copies)])
        copies[key].start()

    for i in range(blocks):
        start(("x", i), xs[i], x_buf.at[pl.ds(i * rows, rows)])
    start(("w", 0), weights[0], w_in.at[:, pl.ds(0, hidden)])
    start(("w", 1), weights[1], w_in.at[:, pl.ds(hidden, hidden)])
    for i in range(blocks):
        start(("g", i), gs[i], g_buf.at[pl.ds(i * rows, rows)])
    start(("w", 2), weights[2], w_out.at[pl.ds(0, hidden)])
    start(("w", 3), weights[3], w_in.at[:, pl.ds(2 * hidden, hidden)])
    start(("w", 4), weights[4], w_in.at[:, pl.ds(3 * hidden, hidden)])
    start(("w", 5), weights[5], w_out.at[pl.ds(hidden, hidden)])
    for i in range(blocks):
        copies["x", i].wait()
    for k in range(2):
        at = 2 * k * hidden
        copies["w", 3 * k].wait()
        pre_gate = jnp.dot(x_buf[...], w_in[:, at : at + hidden], preferred_element_type=F32)
        copies["w", 3 * k + 1].wait()
        pre_up = jnp.dot(x_buf[...], w_in[:, at + hidden : at + 2 * hidden], preferred_element_type=F32)
        if k == 0:
            for i in range(blocks):
                copies["g", i].wait()
        copies["w", 3 * k + 2].wait()
        back = lax.dot_general(
            g_buf[...], w_out[k * hidden : (k + 1) * hidden, :], LAST, preferred_element_type=F32
        )
        gate = [
            gates[pl.ds(pl.multiple_of(order[first + i] * rows, rows), rows), k : k + 1] for i in range(blocks)
        ]
        back = back * jnp.concatenate(gate, axis=0)
        sig = jax.nn.sigmoid(pre_gate)
        back_sig = back * sig
        d_buf[:, at : at + hidden] = (back_sig * pre_up * (1.0 + pre_gate * (1.0 - sig))).astype(BF16)
        d_buf[:, at + hidden : at + 2 * hidden] = (back_sig * pre_gate).astype(BF16)
    for c in range(0, width, wide):
        term = lax.dot_general(d_buf[...], w_in[c : c + wide, :], LAST, preferred_element_type=F32)
        for i, out in enumerate(outs):
            out[:, c : c + wide] = term[i * rows : (i + 1) * rows, :].astype(out.dtype)


def pair_rows(xs, gs, gates, order, first, weights, kinds):
    blocks = len(xs)
    rows, width = xs[0].shape
    hidden = weights[0].shape[1]
    there = pl.BlockSpec(memory_space=pl.ANY)
    near = pl.BlockSpec(memory_space=pltpu.VMEM)
    count = blocks * rows
    return pl.pallas_call(
        partial(pair_kernel, blocks, first, 512 if width % 512 == 0 else width),
        in_specs=[pl.BlockSpec(memory_space=pltpu.SMEM)] + [there] * (2 * blocks) + [near] + [there] * 6,
        out_specs=[near] * blocks,
        out_shape=[jax.ShapeDtypeStruct((rows, width), kind) for kind in kinds],
        scratch_shapes=[
            pltpu.VMEM((count, width), BF16),
            pltpu.VMEM((count, width), BF16),
            pltpu.VMEM((width, 4 * hidden), BF16),
            pltpu.VMEM((2 * hidden, width), BF16),
            pltpu.VMEM((count, 4 * hidden), BF16),
            pltpu.SemaphoreType.DMA((2 * blocks + 6,)),
        ],
        compiler_params=pltpu.CompilerParams(vmem_limit_bytes=40 * 2**20),
        cost_estimate=pl.CostEstimate(
            flops=20 * count * width * hidden,
            bytes_accessed=12 * width * hidden + 7 * count * width,
            transcendentals=2 * count * hidden,
        ),
        name="pair_rows",
    )(order, *xs, *gs, gates, *weights)


def gathered(layer_input, out_grad, expert_ids, gates, w_gate, w_up, w_down):
    owners = lax.axis_size("expert")
    ring = owners // 4
    rows = layer_input.shape[0]
    me = lax.axis_index("expert")
    core, chip = me % 2, me // 2
    y, z = chip % 2, chip // 2

    def turn(value, by):
        return lax.ppermute(value, "expert", [(i, (i + 4 * by) % owners) for i in range(owners)])

    def swap(value, bit):
        return lax.ppermute(value, "expert", [(i, i ^ bit) for i in range(owners)])

    own = (w_gate[0], w_up[0], w_down[0])
    weights = own + tuple(swap(w, 1) for w in own)

    named = expert_ids[:, :, None] == jnp.arange(owners, dtype=jnp.int32)[None, None, :]
    dense = jnp.sum(jnp.where(named, gates[:, :, None], 0.0), axis=1)
    every = lax.all_gather(dense, "expert", tiled=True)
    pair = [jnp.sum(jnp.where(jnp.arange(owners)[None, :] == e, every, 0.0), axis=1) for e in (me, me ^ 1)]
    gate_pair = jnp.stack(pair, axis=1)
    zs = (z - jnp.arange(ring)) % ring
    order = ((zs[:, None] * 2 + jnp.stack([y, 1 - y])[None, :]) * 2 + core).reshape(-1).astype(jnp.int32)

    x_own, g_own = layer_input, out_grad
    total = None
    for s in range(ring):
        if s:
            x_own, g_own = turn(x_own, 1), turn(g_own, 1)
        x_far, g_far = swap(x_own, 2), swap(g_own, 2)
        near, far = pair_rows((x_own, x_far), (g_own, g_far), gate_pair, order, 2 * s, weights, (F32, BF16))
        both = near + swap(far, 2).astype(F32)
        if s:
            both = turn(both.astype(BF16), -s).astype(F32)
        total = both if total is None else total + both
    return total


def expert_rows(rows_in, rows_grad, gate_w, up_w, down_w):
    pre_gate = jnp.dot(rows_in, gate_w, preferred_element_type=F32)
    pre_up = jnp.dot(rows_in, up_w, preferred_element_type=F32)
    back = lax.dot_general(rows_grad, down_w, LAST, preferred_element_type=F32)
    sig = jax.nn.sigmoid(pre_gate)
    d_gate = (back * pre_up * sig * (1.0 + pre_gate * (1.0 - sig))).astype(BF16)
    d_up = (back * pre_gate * sig).astype(BF16)
    term = lax.dot_general(d_gate, gate_w, LAST, preferred_element_type=F32)
    return term + lax.dot_general(d_up, up_w, LAST, preferred_element_type=F32)


def routed(layer_input, out_grad, expert_ids, gates, w_gate, w_up, w_down):
    owners = lax.axis_size("expert")
    rows, width = layer_input.shape
    choose = expert_ids.shape[1]
    capacity = 5 * rows * choose // (4 * owners)
    flat_ids = expert_ids.reshape(-1)
    flat_gates = gates.reshape(-1)
    assigned = flat_ids.shape[0]
    onehot = flat_ids[:, None] == jnp.arange(owners, dtype=jnp.int32)[None, :]
    earlier = jnp.tril(jnp.ones((assigned, assigned), BF16), -1)
    before = jnp.dot(earlier, onehot.astype(BF16), preferred_element_type=F32)
    position = jnp.sum(jnp.where(onehot, before, 0.0), axis=1).astype(jnp.int32)
    slot = flat_ids * capacity + position
    source = jnp.full((owners * capacity,), -1, jnp.int32).at[slot].set(jnp.arange(assigned, dtype=jnp.int32))
    valid = source >= 0
    safe = jnp.maximum(source, 0)
    token = safe // choose
    send_in = jnp.where(valid[:, None], layer_input[token], jnp.zeros((), BF16))
    gate_val = jnp.where(valid, flat_gates[safe], 0.0)
    send_grad = (gate_val[:, None] * out_grad[token].astype(F32)).astype(BF16)

    def exchange(value):
        value = value.reshape(owners, capacity, width)
        value = lax.all_to_all(value, "expert", split_axis=0, concat_axis=0, tiled=True)
        return value.reshape(owners * capacity, width)

    term = expert_rows(exchange(send_in), exchange(send_grad), w_gate[0], w_up[0], w_down[0])
    picked = exchange(term)[slot].reshape(rows, choose, width)
    return jnp.sum(picked, axis=1)


def on_device(layer_input, out_grad, expert_ids, gates, w_gate, w_up, w_down):
    owners = lax.axis_size("expert")
    dense = owners % 4 == 0 and expert_ids.shape[1] * 4 >= owners
    plan = gathered if dense else routed
    return plan(layer_input, out_grad, expert_ids, gates, w_gate, w_up, w_down)


def solution(mesh):
    rows = P(("group", "expert"), None)
    owned = P("expert", None, None)
    return jax.shard_map(
        on_device,
        mesh=mesh,
        in_specs=(rows, rows, rows, rows, owned, owned, owned),
        out_specs=rows,
        check_vma=False,
    )
```

```python
from functools import partial

import jax
import jax.numpy as jnp
from jax import lax
from jax.experimental import pallas as pl
from jax.experimental.pallas import tpu as pltpu
from jax.sharding import PartitionSpec as P

F32 = jnp.float32
BF16 = jnp.bfloat16
LAST = (((1,), (1,)), ((), ()))


def pair_kernel(blocks, wide, experts, *refs):
    sides = refs[:blocks]
    gates = refs[blocks]
    weights = refs[blocks + 1 : blocks + 7]
    outs = refs[blocks + 7 : 2 * blocks + 7]
    x_buf, g_buf, w_in, w_out, d_buf, sems = refs[2 * blocks + 7 :]
    rows = sides[0].shape[0]
    width, hidden = weights[0].shape
    copies = {}

    def start(key, source, target):
        copies[key] = pltpu.make_async_copy(source, target, sems.at[len(copies)])
        copies[key].start()

    for i in range(blocks):
        start(("x", i), sides[i].at[:, pl.ds(0, width)], x_buf.at[pl.ds(i * rows, rows)])
    start(("w", 0), weights[0], w_in.at[:, pl.ds(0, hidden)])
    start(("w", 1), weights[1], w_in.at[:, pl.ds(hidden, hidden)])
    for i in range(blocks):
        start(("g", i), sides[i].at[:, pl.ds(width, width)], g_buf.at[pl.ds(i * rows, rows)])
    start(("w", 2), weights[2], w_out.at[pl.ds(0, hidden)])
    start(("w", 3), weights[3], w_in.at[:, pl.ds(2 * hidden, hidden)])
    start(("w", 4), weights[4], w_in.at[:, pl.ds(3 * hidden, hidden)])
    start(("w", 5), weights[5], w_out.at[pl.ds(hidden, hidden)])
    lanes = lax.broadcasted_iota(jnp.int32, gates.shape, 1)
    for i in range(blocks):
        copies["x", i].wait()
    for k in range(2):
        at = 2 * k * hidden
        copies["w", 3 * k].wait()
        pre_gate = jnp.dot(x_buf[...], w_in[:, at : at + hidden], preferred_element_type=F32)
        copies["w", 3 * k + 1].wait()
        pre_up = jnp.dot(x_buf[...], w_in[:, at + hidden : at + 2 * hidden], preferred_element_type=F32)
        if k == 0:
            for i in range(blocks):
                copies["g", i].wait()
        copies["w", 3 * k + 2].wait()
        back = lax.dot_general(
            g_buf[...], w_out[k * hidden : (k + 1) * hidden, :], LAST, preferred_element_type=F32
        )
        back = back * jnp.sum(jnp.where(lanes == experts[k], gates[...], 0.0), axis=1, keepdims=True)
        sig = jax.nn.sigmoid(pre_gate)
        back_sig = back * sig
        d_buf[:, at : at + hidden] = (back_sig * pre_up * (1.0 + pre_gate * (1.0 - sig))).astype(BF16)
        d_buf[:, at + hidden : at + 2 * hidden] = (back_sig * pre_gate).astype(BF16)
    for c in range(0, width, wide):
        term = lax.dot_general(d_buf[...], w_in[c : c + wide, :], LAST, preferred_element_type=F32)
        for i, out in enumerate(outs):
            out[:, c : c + wide] = term[i * rows : (i + 1) * rows, :].astype(out.dtype)


def pair_rows(sides, gates, experts, weights, kinds):
    blocks = len(sides)
    rows, width = sides[0].shape[0], sides[0].shape[1] // 2
    hidden = weights[0].shape[1]
    there = pl.BlockSpec(memory_space=pltpu.HBM)
    near = pl.BlockSpec(memory_space=pltpu.VMEM)
    count = blocks * rows
    return pl.pallas_call(
        partial(pair_kernel, blocks, 512 if width % 512 == 0 else width),
        in_specs=[pl.BlockSpec(memory_space=pltpu.SMEM)] + [there] * blocks + [near] + [there] * 6,
        out_specs=[near] * blocks,
        out_shape=[jax.ShapeDtypeStruct((rows, width), kind) for kind in kinds],
        scratch_shapes=[
            pltpu.VMEM((count, width), BF16),
            pltpu.VMEM((count, width), BF16),
            pltpu.VMEM((width, 4 * hidden), BF16),
            pltpu.VMEM((2 * hidden, width), BF16),
            pltpu.VMEM((count, 4 * hidden), BF16),
            pltpu.SemaphoreType.DMA((2 * blocks + 6,)),
        ],
        compiler_params=pltpu.CompilerParams(vmem_limit_bytes=60 * 2**20),
        cost_estimate=pl.CostEstimate(
            flops=20 * count * width * hidden,
            bytes_accessed=12 * width * hidden + 7 * count * width,
            transcendentals=2 * count * hidden,
        ),
        name="pair_rows",
    )(experts, *sides, gates, *weights)


def gathered(layer_input, out_grad, expert_ids, gates, w_gate, w_up, w_down):
    owners = lax.axis_size("expert")
    ring = owners // 4
    me = lax.axis_index("expert")

    def turn(value, by):
        return lax.ppermute(value, "expert", [(i, (i + 4 * by) % owners) for i in range(owners)])

    def swap(value, bit):
        return lax.ppermute(value, "expert", [(i, i ^ bit) for i in range(owners)])

    own = (w_gate[0], w_up[0], w_down[0])
    weights = own + tuple(swap(w, 1) for w in own)
    experts = jnp.stack([me, me ^ 1]).astype(jnp.int32)

    named = expert_ids[:, :, None] == jnp.arange(owners, dtype=jnp.int32)[None, None, :]
    dense = jnp.sum(jnp.where(named, gates[:, :, None], 0.0), axis=1)
    pair_gates = jnp.concatenate([dense, swap(dense, 2)], axis=0)

    near_side = jnp.concatenate([layer_input, out_grad], axis=1)
    step_gates = [pair_gates]
    held, parts = [], []
    for s in range(ring):
        far_side = swap(near_side, 2)
        next_side = turn(near_side, 1) if s + 1 < ring else None
        if s == 0:
            far_side, next_side, weights, step_gates = lax.optimization_barrier(
                (far_side, next_side, weights, step_gates)
            )
        else:
            if s == 1:
                step_gates = step_gates + [turn(step_gates[0], by) for by in range(1, ring)]
            near, far = pair_rows(held, step_gates[s - 1], experts, weights, (F32, BF16))
            far = swap(far, 2)
            far_side, next_side, step_gates, near = lax.optimization_barrier((far_side, next_side, step_gates, near))
            parts.append((near, far))
        held = [near_side, far_side]
        near_side = next_side
    near, far = pair_rows(held, step_gates[ring - 1], experts, weights, (F32, BF16))
    parts.append((near, swap(far, 2)))
    total = None
    for s, (near, far) in enumerate(parts):
        both = near + far.astype(F32)
        if s:
            both = turn(both.astype(BF16), -s).astype(F32)
        total = both if total is None else total + both
    return total


def expert_rows(rows_in, rows_grad, gate_w, up_w, down_w):
    pre_gate = jnp.dot(rows_in, gate_w, preferred_element_type=F32)
    pre_up = jnp.dot(rows_in, up_w, preferred_element_type=F32)
    back = lax.dot_general(rows_grad, down_w, LAST, preferred_element_type=F32)
    sig = jax.nn.sigmoid(pre_gate)
    d_gate = (back * pre_up * sig * (1.0 + pre_gate * (1.0 - sig))).astype(BF16)
    d_up = (back * pre_gate * sig).astype(BF16)
    term = lax.dot_general(d_gate, gate_w, LAST, preferred_element_type=F32)
    return term + lax.dot_general(d_up, up_w, LAST, preferred_element_type=F32)


def routed(layer_input, out_grad, expert_ids, gates, w_gate, w_up, w_down):
    owners = lax.axis_size("expert")
    rows, width = layer_input.shape
    choose = expert_ids.shape[1]
    capacity = 5 * rows * choose // (4 * owners)
    flat_ids = expert_ids.reshape(-1)
    flat_gates = gates.reshape(-1)
    assigned = flat_ids.shape[0]
    onehot = flat_ids[:, None] == jnp.arange(owners, dtype=jnp.int32)[None, :]
    earlier = jnp.tril(jnp.ones((assigned, assigned), BF16), -1)
    before = jnp.dot(earlier, onehot.astype(BF16), preferred_element_type=F32)
    position = jnp.sum(jnp.where(onehot, before, 0.0), axis=1).astype(jnp.int32)
    slot = flat_ids * capacity + position
    source = jnp.full((owners * capacity,), -1, jnp.int32).at[slot].set(jnp.arange(assigned, dtype=jnp.int32))
    valid = source >= 0
    safe = jnp.maximum(source, 0)
    token = safe // choose
    send_in = jnp.where(valid[:, None], layer_input[token], jnp.zeros((), BF16))
    gate_val = jnp.where(valid, flat_gates[safe], 0.0)
    send_grad = (gate_val[:, None] * out_grad[token].astype(F32)).astype(BF16)

    def exchange(value):
        value = value.reshape(owners, capacity, width)
        value = lax.all_to_all(value, "expert", split_axis=0, concat_axis=0, tiled=True)
        return value.reshape(owners * capacity, width)

    term = expert_rows(exchange(send_in), exchange(send_grad), w_gate[0], w_up[0], w_down[0])
    picked = exchange(term)[slot].reshape(rows, choose, width)
    return jnp.sum(picked, axis=1)


def on_device(layer_input, out_grad, expert_ids, gates, w_gate, w_up, w_down):
    owners = lax.axis_size("expert")
    dense = owners % 4 == 0 and expert_ids.shape[1] * 4 >= owners
    plan = gathered if dense else routed
    return plan(layer_input, out_grad, expert_ids, gates, w_gate, w_up, w_down)


def solution(mesh):
    rows = P(("group", "expert"), None)
    owned = P("expert", None, None)
    return jax.shard_map(
        on_device,
        mesh=mesh,
        in_specs=(rows, rows, rows, rows, owned, owned, owned),
        out_specs=rows,
        check_vma=False,
    )
```

```python
from functools import partial

import jax
import jax.numpy as jnp
from jax import lax
from jax.experimental import pallas as pl
from jax.experimental.pallas import tpu as pltpu
from jax.sharding import PartitionSpec as P

F32 = jnp.float32
BF16 = jnp.bfloat16
LAST = (((1,), (1,)), ((), ()))


def pair_kernel(blocks, owners, wide, experts, *refs):
    xs, gs = refs[:blocks], refs[blocks : 2 * blocks]
    weights = refs[2 * blocks : 2 * blocks + 6]
    outs = refs[2 * blocks + 6 : 3 * blocks + 6]
    x_buf, g_buf, w_in, w_out, d_buf, sems = refs[3 * blocks + 6 :]
    rows = xs[0].shape[0]
    width, hidden = weights[0].shape
    copies = {}

    def start(key, source, target):
        copies[key] = pltpu.make_async_copy(source, target, sems.at[len(copies)])
        copies[key].start()

    for i in range(blocks):
        start(("x", i), xs[i], x_buf.at[pl.ds(i * rows, rows)])
    start(("w", 0), weights[0], w_in.at[:, pl.ds(0, hidden)])
    start(("w", 1), weights[1], w_in.at[:, pl.ds(hidden, hidden)])
    for i in range(blocks):
        start(("g", i), gs[i], g_buf.at[pl.ds(i * rows, rows)])
    start(("w", 2), weights[2], w_out.at[pl.ds(0, hidden)])
    start(("w", 3), weights[3], w_in.at[:, pl.ds(2 * hidden, hidden)])
    start(("w", 4), weights[4], w_in.at[:, pl.ds(3 * hidden, hidden)])
    start(("w", 5), weights[5], w_out.at[pl.ds(hidden, hidden)])
    for i in range(blocks):
        copies["x", i].wait()
    for k in range(2):
        at = 2 * k * hidden
        copies["w", 3 * k].wait()
        pre_gate = jnp.dot(x_buf[...], w_in[:, at : at + hidden], preferred_element_type=F32)
        copies["w", 3 * k + 1].wait()
        pre_up = jnp.dot(x_buf[...], w_in[:, at + hidden : at + 2 * hidden], preferred_element_type=F32)
        if k == 0:
            for i in range(blocks):
                copies["g", i].wait()
            pieces = g_buf[:, width:].astype(F32)
            lane = lax.broadcasted_iota(jnp.int32, pieces.shape, 1)
        chosen = (lane == experts[k]) | (lane == experts[k] + owners) | (lane == experts[k] + 2 * owners)
        gate = jnp.sum(jnp.where(chosen, pieces, 0.0), axis=1, keepdims=True)
        scaled = (gate * g_buf[:, :width].astype(F32)).astype(BF16)
        copies["w", 3 * k + 2].wait()
        back = lax.dot_general(
            scaled, w_out[k * hidden : (k + 1) * hidden, :], LAST, preferred_element_type=F32
        )
        sig = jax.nn.sigmoid(pre_gate)
        back_sig = back * sig
        d_buf[:, at : at + hidden] = (back_sig * pre_up * (1.0 + pre_gate * (1.0 - sig))).astype(BF16)
        d_buf[:, at + hidden : at + 2 * hidden] = (back_sig * pre_gate).astype(BF16)
    for c in range(0, width, wide):
        term = lax.dot_general(d_buf[...], w_in[c : c + wide, :], LAST, preferred_element_type=F32)
        for i, out in enumerate(outs):
            out[:, c : c + wide] = term[i * rows : (i + 1) * rows, :].astype(out.dtype)


def pair_rows(xs, gs, owners, experts, weights, kinds):
    blocks = len(xs)
    rows, width = xs[0].shape
    hidden = weights[0].shape[1]
    there = pl.BlockSpec(memory_space=pltpu.HBM)
    near = pl.BlockSpec(memory_space=pltpu.VMEM)
    count = blocks * rows
    return pl.pallas_call(
        partial(pair_kernel, blocks, owners, 512 if width % 512 == 0 else width),
        in_specs=[pl.BlockSpec(memory_space=pltpu.SMEM)] + [there] * (2 * blocks + 6),
        out_specs=[near] * blocks,
        out_shape=[jax.ShapeDtypeStruct((rows, width), kind) for kind in kinds],
        scratch_shapes=[
            pltpu.VMEM((count, width), BF16),
            pltpu.VMEM((count, gs[0].shape[1]), BF16),
            pltpu.VMEM((width, 4 * hidden), BF16),
            pltpu.VMEM((2 * hidden, width), BF16),
            pltpu.VMEM((count, 4 * hidden), BF16),
            pltpu.SemaphoreType.DMA((2 * blocks + 6,)),
        ],
        compiler_params=pltpu.CompilerParams(vmem_limit_bytes=60 * 2**20),
        cost_estimate=pl.CostEstimate(
            flops=20 * count * width * hidden,
            bytes_accessed=12 * width * hidden + 7 * count * width,
            transcendentals=2 * count * hidden,
        ),
        name="pair_rows",
    )(experts, *xs, *gs, *weights)


def gathered(layer_input, out_grad, expert_ids, gates, w_gate, w_up, w_down):
    owners = lax.axis_size("expert")
    ring = owners // 4
    rows = layer_input.shape[0]
    me = lax.axis_index("expert")
    experts = jnp.stack([me, me ^ 1]).astype(jnp.int32)

    def turn(value, by):
        return lax.ppermute(value, "expert", [(i, (i + 4 * by) % owners) for i in range(owners)])

    def swap(value, bit):
        return lax.ppermute(value, "expert", [(i, i ^ bit) for i in range(owners)])

    named = expert_ids[:, :, None] == jnp.arange(owners, dtype=jnp.int32)[None, None, :]
    rest = jnp.sum(jnp.where(named, gates[:, :, None], 0.0), axis=1)
    parts = []
    for _ in range(3):
        part = lax.reduce_precision(rest, 8, 7)
        rest = rest - part
        parts.append(part.astype(BF16))
    spare = jnp.zeros((rows, -3 * owners % 128), BF16)

    own = (w_gate[0], w_up[0], w_down[0])
    weights = own + tuple(swap(w, 1) for w in own)

    def rows_of(xs, gs, kinds=(F32, BF16)):
        return pair_rows(xs, gs, owners, experts, weights, kinds)

    xs, gs = [layer_input], [jnp.concatenate([out_grad, *parts, spare], axis=1)]
    far_xs, far_gs, nears, fars = [], [], [], []
    tie = lax.optimization_barrier

    def compute(s):
        near, far = rows_of((xs[s], far_xs[s]), (gs[s], far_gs[s]))
        nears.append(near)
        fars.append(swap(far, 2))

    for s in range(ring - 1):
        far_x, next_x = tie((swap(xs[s], 2), turn(xs[s], 1)))
        far_g, next_g = swap(gs[s], 2), turn(gs[s], 1)
        last_x = turn(far_xs[0], -1) if s and s == max(1, ring - 3) else None
        last_g = turn(far_gs[0], -1) if s and s == ring - 2 else None
        if s == 0:
            far_g, next_g, weights = tie((far_g, next_g, weights))
        else:
            compute(s - 1)
            if s < ring - 2:
                far_g, next_g, nears[s - 1], last_x = tie((far_g, next_g, nears[s - 1], last_x))
            else:
                far_g, nears[s - 1], fars[: s - 1] = tie((far_g, nears[s - 1], fars[: s - 1]))
        far_xs.append(far_x)
        far_gs.append(far_g)
        if s and s == ring - 2:
            compute(s)
            next_x, next_g, last_x, last_g, nears[s], fars[s - 1] = tie(
                (next_x, next_g, last_x if last_x is not None else kept_x, last_g, nears[s], fars[s - 1])
            )
        xs.append(next_x)
        gs.append(next_g)
        kept_x = last_x
    if ring == 1:
        last_x, last_g = swap(xs[0], 2), swap(gs[0], 2)
    elif ring == 2:
        last_x, last_g = turn(far_xs[0], -1), turn(far_gs[0], -1)
        compute(0)
    far_xs.append(last_x)
    far_gs.append(last_g)
    compute(ring - 1)
    sums = [near + far.astype(F32) for near, far in zip(nears, fars)]

    total = sums[0]
    carried = None
    for s in range(ring - 2, 0, -1):
        carried = sums[s] if carried is None else sums[s] + carried
        carried = turn(carried.astype(BF16), -1).astype(F32)
    if ring > 1:
        total = total + turn(sums[ring - 1].astype(BF16), 1).astype(F32)
    return total if carried is None else total + carried


def expert_rows(rows_in, rows_grad, gate_w, up_w, down_w):
    pre_gate = jnp.dot(rows_in, gate_w, preferred_element_type=F32)
    pre_up = jnp.dot(rows_in, up_w, preferred_element_type=F32)
    back = lax.dot_general(rows_grad, down_w, LAST, preferred_element_type=F32)
    sig = jax.nn.sigmoid(pre_gate)
    d_gate = (back * pre_up * sig * (1.0 + pre_gate * (1.0 - sig))).astype(BF16)
    d_up = (back * pre_gate * sig).astype(BF16)
    term = lax.dot_general(d_gate, gate_w, LAST, preferred_element_type=F32)
    return term + lax.dot_general(d_up, up_w, LAST, preferred_element_type=F32)


def routed(layer_input, out_grad, expert_ids, gates, w_gate, w_up, w_down):
    owners = lax.axis_size("expert")
    rows, width = layer_input.shape
    choose = expert_ids.shape[1]
    capacity = 5 * rows * choose // (4 * owners)
    flat_ids = expert_ids.reshape(-1)
    flat_gates = gates.reshape(-1)
    assigned = flat_ids.shape[0]
    onehot = flat_ids[:, None] == jnp.arange(owners, dtype=jnp.int32)[None, :]
    earlier = jnp.tril(jnp.ones((assigned, assigned), BF16), -1)
    before = jnp.dot(earlier, onehot.astype(BF16), preferred_element_type=F32)
    position = jnp.sum(jnp.where(onehot, before, 0.0), axis=1).astype(jnp.int32)
    slot = flat_ids * capacity + position
    source = jnp.full((owners * capacity,), -1, jnp.int32).at[slot].set(jnp.arange(assigned, dtype=jnp.int32))
    valid = source >= 0
    safe = jnp.maximum(source, 0)
    token = safe // choose
    send_in = jnp.where(valid[:, None], layer_input[token], jnp.zeros((), BF16))
    gate_val = jnp.where(valid, flat_gates[safe], 0.0)
    send_grad = (gate_val[:, None] * out_grad[token].astype(F32)).astype(BF16)

    def exchange(value):
        value = value.reshape(owners, capacity, width)
        value = lax.all_to_all(value, "expert", split_axis=0, concat_axis=0, tiled=True)
        return value.reshape(owners * capacity, width)

    term = expert_rows(exchange(send_in), exchange(send_grad), w_gate[0], w_up[0], w_down[0])
    picked = exchange(term)[slot].reshape(rows, choose, width)
    return jnp.sum(picked, axis=1)


def on_device(layer_input, out_grad, expert_ids, gates, w_gate, w_up, w_down):
    owners = lax.axis_size("expert")
    dense = owners % 4 == 0 and expert_ids.shape[1] * 4 >= owners
    plan = gathered if dense else routed
    return plan(layer_input, out_grad, expert_ids, gates, w_gate, w_up, w_down)


def solution(mesh):
    rows = P(("group", "expert"), None)
    owned = P("expert", None, None)
    return jax.shard_map(
        on_device,
        mesh=mesh,
        in_specs=(rows, rows, rows, rows, owned, owned, owned),
        out_specs=rows,
        check_vma=False,
    )
```

```python
from functools import partial

import jax
import jax.numpy as jnp
from jax import lax
from jax.experimental import pallas as pl
from jax.experimental.pallas import tpu as pltpu
from jax.sharding import PartitionSpec as P

F32 = jnp.float32
BF16 = jnp.bfloat16
LAST = (((1,), (1,)), ((), ()))


def pair_kernel(blocks, owners, wide, experts, *refs):
    xs, gs = refs[:blocks], refs[blocks : 2 * blocks]
    weights = refs[2 * blocks : 2 * blocks + 6]
    outs = refs[2 * blocks + 6 : 3 * blocks + 6]
    x_buf, g_buf, w_in, w_out, d_buf, sems = refs[3 * blocks + 6 :]
    rows = xs[0].shape[0]
    width, hidden = weights[0].shape
    copies = {}

    def start(key, source, target):
        copies[key] = pltpu.make_async_copy(source, target, sems.at[len(copies)])
        copies[key].start()

    for i in range(blocks):
        start(("x", i), xs[i], x_buf.at[pl.ds(i * rows, rows)])
    start(("w", 0), weights[0], w_in.at[:, pl.ds(0, hidden)])
    start(("w", 1), weights[1], w_in.at[:, pl.ds(hidden, hidden)])
    for i in range(blocks):
        start(("g", i), gs[i], g_buf.at[pl.ds(i * rows, rows)])
    start(("w", 2), weights[2], w_out.at[pl.ds(0, hidden)])
    start(("w", 3), weights[3], w_in.at[:, pl.ds(2 * hidden, hidden)])
    start(("w", 4), weights[4], w_in.at[:, pl.ds(3 * hidden, hidden)])
    start(("w", 5), weights[5], w_out.at[pl.ds(hidden, hidden)])
    for i in range(blocks):
        copies["x", i].wait()
    for k in range(2):
        at = 2 * k * hidden
        copies["w", 3 * k].wait()
        pre_gate = jnp.dot(x_buf[...], w_in[:, at : at + hidden], preferred_element_type=F32)
        copies["w", 3 * k + 1].wait()
        pre_up = jnp.dot(x_buf[...], w_in[:, at + hidden : at + 2 * hidden], preferred_element_type=F32)
        if k == 0:
            for i in range(blocks):
                copies["g", i].wait()
            pieces = g_buf[:, width:].astype(F32)
            lane = lax.broadcasted_iota(jnp.int32, pieces.shape, 1)
        chosen = (lane == experts[k]) | (lane == experts[k] + owners) | (lane == experts[k] + 2 * owners)
        gate = jnp.sum(jnp.where(chosen, pieces, 0.0), axis=1, keepdims=True)
        scaled = (gate * g_buf[:, :width].astype(F32)).astype(BF16)
        copies["w", 3 * k + 2].wait()
        back = lax.dot_general(
            scaled, w_out[k * hidden : (k + 1) * hidden, :], LAST, preferred_element_type=F32
        )
        sig = jax.nn.sigmoid(pre_gate)
        back_sig = back * sig
        d_buf[:, at : at + hidden] = (back_sig * pre_up * (1.0 + pre_gate * (1.0 - sig))).astype(BF16)
        d_buf[:, at + hidden : at + 2 * hidden] = (back_sig * pre_gate).astype(BF16)
    for c in range(0, width, wide):
        term = lax.dot_general(d_buf[...], w_in[c : c + wide, :], LAST, preferred_element_type=F32)
        for i, out in enumerate(outs):
            out[:, c : c + wide] = term[i * rows : (i + 1) * rows, :].astype(out.dtype)


def pair_rows(xs, gs, owners, experts, weights, kinds):
    blocks = len(xs)
    rows, width = xs[0].shape
    hidden = weights[0].shape[1]
    there = pl.BlockSpec(memory_space=pltpu.HBM)
    near = pl.BlockSpec(memory_space=pltpu.VMEM)
    count = blocks * rows
    return pl.pallas_call(
        partial(pair_kernel, blocks, owners, 512 if width % 512 == 0 else width),
        in_specs=[pl.BlockSpec(memory_space=pltpu.SMEM)] + [there] * (2 * blocks) + [pl.BlockSpec(memory_space=pl.ANY)] * 6,
        out_specs=[near] * blocks,
        out_shape=[jax.ShapeDtypeStruct((rows, width), kind) for kind in kinds],
        scratch_shapes=[
            pltpu.VMEM((count, width), BF16),
            pltpu.VMEM((count, gs[0].shape[1]), BF16),
            pltpu.VMEM((width, 4 * hidden), BF16),
            pltpu.VMEM((2 * hidden, width), BF16),
            pltpu.VMEM((count, 4 * hidden), BF16),
            pltpu.SemaphoreType.DMA((2 * blocks + 6,)),
        ],
        compiler_params=pltpu.CompilerParams(vmem_limit_bytes=36 * 2**20),
        cost_estimate=pl.CostEstimate(
            flops=20 * count * width * hidden,
            bytes_accessed=12 * width * hidden + 7 * count * width,
            transcendentals=2 * count * hidden,
        ),
        name="pair_rows",
    )(experts, *xs, *gs, *weights)


def gathered(layer_input, out_grad, expert_ids, gates, w_gate, w_up, w_down):
    owners = lax.axis_size("expert")
    ring = owners // 4
    rows = layer_input.shape[0]
    me = lax.axis_index("expert")
    experts = jnp.stack([me, me ^ 1]).astype(jnp.int32)

    def turn(value, by):
        return lax.ppermute(value, "expert", [(i, (i + 4 * by) % owners) for i in range(owners)])

    def swap(value, bit):
        return lax.ppermute(value, "expert", [(i, i ^ bit) for i in range(owners)])

    tie = lax.optimization_barrier

    named = expert_ids[:, :, None] == jnp.arange(owners, dtype=jnp.int32)[None, None, :]
    rest = jnp.sum(jnp.where(named, gates[:, :, None], 0.0), axis=1)
    parts = []
    for _ in range(3):
        part = lax.reduce_precision(rest, 8, 7)
        rest = rest - part
        parts.append(part.astype(BF16))
    spare = jnp.zeros((rows, -3 * owners % 128), BF16)

    own = (w_gate[0], w_up[0], w_down[0])

    x, g = tie((layer_input, jnp.concatenate([out_grad, *parts, spare], axis=1)))
    xs, gs = [x], [g]
    far_xs, far_gs, nears, fars = [], [], [], []

    def compute(s):
        return pair_rows(
            (xs[s], far_xs[s]), (gs[s], far_gs[s]), owners, experts, weights, (F32, BF16)
        )

    for s in range(ring - 2):
        far_x, x, far_g, g = swap(xs[s], 2), turn(xs[s], 1), swap(gs[s], 2), turn(gs[s], 1)
        if s == 0:
            theirs = [swap(own[0], 1)]
            sent, far_x, x, theirs = tie((own[1:], far_x, x, theirs))
            far_g, g, theirs = tie((far_g, g, theirs + [swap(w, 1) for w in sent]))
            weights = (*own, *theirs)
        else:
            near, far = compute(s - 1)
            far_x, x = tie((far_x, x))
            far_g, g, near = tie((far_g, g, near))
            nears.append(near)
            fars.append(far)
        xs, gs, far_xs, far_gs = xs + [x], gs + [g], far_xs + [far_x], far_gs + [far_g]

    beyond_x, beyond_g = turn(far_xs[0], -1), turn(far_gs[0], -1)
    x, beyond_x = tie((xs[-1], beyond_x))
    x = turn(x, 1)
    g, beyond_g = tie((gs[-1], beyond_g))
    g = turn(g, 1)
    near, far = compute(ring - 3)
    far_x, far_g, near, beyond_x, beyond_g = tie((swap(xs[-1], 2), swap(gs[-1], 2), near, beyond_x, beyond_g))
    far_xs, far_gs, nears, fars = far_xs + [far_x], far_gs + [far_g], nears + [near], fars + [far]
    backs = [swap(far, 2) for far in fars[1:]]
    near, far = compute(ring - 2)
    near, far, beyond_x, x, backs = tie((near, far, beyond_x, x, backs))
    (beyond,) = pair_rows((beyond_x,), (beyond_g,), owners, experts, weights, (BF16,))
    sums = [None, *(near + back.astype(F32) for near, back in zip(nears[1:] + [near], backs + [swap(far, 2)]))]
    one, carried = turn(sums[1].astype(BF16), -1), sums[2].astype(BF16)
    x, g, first, carried, beyond = tie((x, g, fars[0], carried, beyond))
    (last,) = pair_rows((x,), (g,), owners, experts, weights, (F32,))
    last, one = tie((last, one))

    for s in range(3, ring):
        carried = turn(carried, 1).astype(F32)
        if s < ring - 1:
            carried = (sums[s] + carried).astype(BF16)
    last = (last + swap(beyond, 2).astype(F32) + carried).astype(BF16)
    total = nears[0] + swap(first, 2).astype(F32)
    return total + turn(last, 1).astype(F32) + one.astype(F32)


def expert_rows(rows_in, rows_grad, gate_w, up_w, down_w):
    pre_gate = jnp.dot(rows_in, gate_w, preferred_element_type=F32)
    pre_up = jnp.dot(rows_in, up_w, preferred_element_type=F32)
    back = lax.dot_general(rows_grad, down_w, LAST, preferred_element_type=F32)
    sig = jax.nn.sigmoid(pre_gate)
    d_gate = (back * pre_up * sig * (1.0 + pre_gate * (1.0 - sig))).astype(BF16)
    d_up = (back * pre_gate * sig).astype(BF16)
    term = lax.dot_general(d_gate, gate_w, LAST, preferred_element_type=F32)
    return term + lax.dot_general(d_up, up_w, LAST, preferred_element_type=F32)


def routed(layer_input, out_grad, expert_ids, gates, w_gate, w_up, w_down):
    owners = lax.axis_size("expert")
    rows, width = layer_input.shape
    choose = expert_ids.shape[1]
    capacity = 5 * rows * choose // (4 * owners)
    flat_ids = expert_ids.reshape(-1)
    flat_gates = gates.reshape(-1)
    assigned = flat_ids.shape[0]
    onehot = flat_ids[:, None] == jnp.arange(owners, dtype=jnp.int32)[None, :]
    earlier = jnp.tril(jnp.ones((assigned, assigned), BF16), -1)
    before = jnp.dot(earlier, onehot.astype(BF16), preferred_element_type=F32)
    position = jnp.sum(jnp.where(onehot, before, 0.0), axis=1).astype(jnp.int32)
    slot = flat_ids * capacity + position
    source = jnp.full((owners * capacity,), -1, jnp.int32).at[slot].set(jnp.arange(assigned, dtype=jnp.int32))
    valid = source >= 0
    safe = jnp.maximum(source, 0)
    token = safe // choose
    send_in = jnp.where(valid[:, None], layer_input[token], jnp.zeros((), BF16))
    gate_val = jnp.where(valid, flat_gates[safe], 0.0)
    send_grad = (gate_val[:, None] * out_grad[token].astype(F32)).astype(BF16)

    def exchange(value):
        value = value.reshape(owners, capacity, width)
        value = lax.all_to_all(value, "expert", split_axis=0, concat_axis=0, tiled=True)
        return value.reshape(owners * capacity, width)

    term = expert_rows(exchange(send_in), exchange(send_grad), w_gate[0], w_up[0], w_down[0])
    picked = exchange(term)[slot].reshape(rows, choose, width)
    return jnp.sum(picked, axis=1)


def on_device(layer_input, out_grad, expert_ids, gates, w_gate, w_up, w_down):
    owners = lax.axis_size("expert")
    dense = owners % 4 == 0 and owners >= 16 and expert_ids.shape[1] * 4 >= owners
    plan = gathered if dense else routed
    return plan(layer_input, out_grad, expert_ids, gates, w_gate, w_up, w_down)


def solution(mesh):
    rows = P(("group", "expert"), None)
    owned = P("expert", None, None)
    return jax.shard_map(
        on_device,
        mesh=mesh,
        in_specs=(rows, rows, rows, rows, owned, owned, owned),
        out_specs=rows,
        check_vma=False,
    )
```

```python
from functools import partial

import jax
import jax.numpy as jnp
from jax import lax
from jax.experimental import pallas as pl
from jax.experimental.pallas import tpu as pltpu
from jax.sharding import PartitionSpec as P

F32 = jnp.float32
BF16 = jnp.bfloat16
LAST = (((1,), (1,)), ((), ()))


def gated_kernel(owners, ids, gates, grad, out):
    width = grad.shape[1]
    out[:, :width] = grad[...]
    lane = lax.broadcasted_iota(jnp.int32, (out.shape[1] - width, grad.shape[0]), 0)
    expert = lax.rem(lane, owners)
    high = jnp.zeros(lane.shape, F32)
    for k in range(ids.shape[0]):
        high = jnp.where(ids[k : k + 1, :] == expert, gates[k : k + 1, :], high)
    low = high - high.astype(BF16).astype(F32)
    lowest = low - low.astype(BF16).astype(F32)
    parts = jnp.where(lane < owners, high, jnp.where(lane < 2 * owners, low, lowest))
    parts = jnp.where(lane < 3 * owners, parts, 0.0)
    out[:, width:] = parts.T.astype(BF16)


def gated_rows(grad, ids, gates, owners):
    rows, width = grad.shape
    near = pl.BlockSpec(memory_space=pltpu.VMEM)
    return pl.pallas_call(
        partial(gated_kernel, owners),
        in_specs=[near] * 3,
        out_specs=near,
        out_shape=jax.ShapeDtypeStruct((rows, width + -(-3 * owners // 128) * 128), BF16),
        name="gated_rows",
    )(ids.T, gates.T, grad)


def pair_kernel(blocks, owners, wide, experts, *refs):
    xs, gs = refs[:blocks], refs[blocks : 2 * blocks]
    weights = refs[2 * blocks : 2 * blocks + 6]
    outs = refs[2 * blocks + 6 : 3 * blocks + 6]
    x_buf, g_buf, w_in, w_out, d_buf, sems = refs[3 * blocks + 6 :]
    rows = xs[0].shape[0]
    width, hidden = weights[0].shape
    copies = {}

    def start(key, source, target):
        copies[key] = pltpu.make_async_copy(source, target, sems.at[len(copies)])
        copies[key].start()

    for i in range(blocks):
        start(("x", i), xs[i], x_buf.at[pl.ds(i * rows, rows)])
    start(("w", 0), weights[0], w_in.at[:, pl.ds(0, hidden)])
    start(("w", 1), weights[1], w_in.at[:, pl.ds(hidden, hidden)])
    for i in range(blocks):
        start(("g", i), gs[i], g_buf.at[pl.ds(i * rows, rows)])
    start(("w", 2), weights[2], w_out.at[pl.ds(0, hidden)])
    start(("w", 3), weights[3], w_in.at[:, pl.ds(2 * hidden, hidden)])
    start(("w", 4), weights[4], w_in.at[:, pl.ds(3 * hidden, hidden)])
    start(("w", 5), weights[5], w_out.at[pl.ds(hidden, hidden)])
    for i in range(blocks):
        copies["x", i].wait()
    for k in range(2):
        at = 2 * k * hidden
        copies["w", 3 * k].wait()
        pre_gate = jnp.dot(x_buf[...], w_in[:, at : at + hidden], preferred_element_type=F32)
        copies["w", 3 * k + 1].wait()
        pre_up = jnp.dot(x_buf[...], w_in[:, at + hidden : at + 2 * hidden], preferred_element_type=F32)
        if k == 0:
            for i in range(blocks):
                copies["g", i].wait()
            pieces = g_buf[:, width:].astype(F32)
            lane = lax.broadcasted_iota(jnp.int32, pieces.shape, 1)
        chosen = (lane == experts[k]) | (lane == experts[k] + owners) | (lane == experts[k] + 2 * owners)
        gate = jnp.sum(jnp.where(chosen, pieces, 0.0), axis=1, keepdims=True)
        scaled = (gate * g_buf[:, :width].astype(F32)).astype(BF16)
        copies["w", 3 * k + 2].wait()
        back = lax.dot_general(
            scaled, w_out[k * hidden : (k + 1) * hidden, :], LAST, preferred_element_type=F32
        )
        sig = jax.nn.sigmoid(pre_gate)
        back_sig = back * sig
        d_buf[:, at : at + hidden] = (back_sig * pre_up * (1.0 + pre_gate * (1.0 - sig))).astype(BF16)
        d_buf[:, at + hidden : at + 2 * hidden] = (back_sig * pre_gate).astype(BF16)
    for c in range(0, width, wide):
        term = lax.dot_general(d_buf[...], w_in[c : c + wide, :], LAST, preferred_element_type=F32)
        for i, out in enumerate(outs):
            out[:, c : c + wide] = term[i * rows : (i + 1) * rows, :].astype(out.dtype)


def pair_rows(xs, gs, owners, experts, weights, kinds):
    blocks = len(xs)
    rows, width = xs[0].shape
    hidden = weights[0].shape[1]
    there = pl.BlockSpec(memory_space=pltpu.HBM)
    near = pl.BlockSpec(memory_space=pltpu.VMEM)
    count = blocks * rows
    return pl.pallas_call(
        partial(pair_kernel, blocks, owners, 512 if width % 512 == 0 else width),
        in_specs=[pl.BlockSpec(memory_space=pltpu.SMEM)] + [there] * (2 * blocks) + [pl.BlockSpec(memory_space=pl.ANY)] * 6,
        out_specs=[near] * blocks,
        out_shape=[jax.ShapeDtypeStruct((rows, width), kind) for kind in kinds],
        scratch_shapes=[
            pltpu.VMEM((count, width), BF16),
            pltpu.VMEM((count, gs[0].shape[1]), BF16),
            pltpu.VMEM((width, 4 * hidden), BF16),
            pltpu.VMEM((2 * hidden, width), BF16),
            pltpu.VMEM((count, 4 * hidden), BF16),
            pltpu.SemaphoreType.DMA((2 * blocks + 6,)),
        ],
        compiler_params=pltpu.CompilerParams(vmem_limit_bytes=36 * 2**20),
        cost_estimate=pl.CostEstimate(
            flops=20 * count * width * hidden,
            bytes_accessed=12 * width * hidden + 7 * count * width,
            transcendentals=2 * count * hidden,
        ),
        name="pair_rows",
    )(experts, *xs, *gs, *weights)


def gathered(layer_input, out_grad, expert_ids, gates, w_gate, w_up, w_down):
    owners = lax.axis_size("expert")
    ring = owners // 4
    me = lax.axis_index("expert")
    experts = jnp.stack([me, me ^ 1]).astype(jnp.int32)

    def turn(value, by):
        return lax.ppermute(value, "expert", [(i, (i + 4 * by) % owners) for i in range(owners)])

    def swap(value, bit):
        return lax.ppermute(value, "expert", [(i, i ^ bit) for i in range(owners)])

    tie = lax.optimization_barrier

    own = (w_gate[0], w_up[0], w_down[0])

    xs, gs = [layer_input], [gated_rows(out_grad, expert_ids, gates, owners)]
    far_xs, far_gs, nears, fars = [], [], [], []

    def compute(s):
        return pair_rows(
            (xs[s], far_xs[s]), (gs[s], far_gs[s]), owners, experts, weights, (F32, BF16)
        )

    for s in range(ring - 2):
        far_x, x, far_g, g = swap(xs[s], 2), turn(xs[s], 1), swap(gs[s], 2), turn(gs[s], 1)
        if s == 0:
            theirs, sent = [swap(own[0], 1)], own[1:]
            far_x, x, far_g, g, theirs, sent = tie((far_x, x, far_g, g, theirs, sent))
            weights = (*own, *theirs, *(swap(w, 1) for w in sent))
        else:
            near, far = compute(s - 1)
            far_x, x = tie((far_x, x))
            far_g, g, near = tie((far_g, g, near))
            nears.append(near)
            fars.append(far)
        xs, gs, far_xs, far_gs = xs + [x], gs + [g], far_xs + [far_x], far_gs + [far_g]

    beyond_x, beyond_g = turn(far_xs[0], -1), turn(far_gs[0], -1)
    x, beyond_x = tie((xs[-1], beyond_x))
    x = turn(x, 1)
    g, beyond_g = tie((gs[-1], beyond_g))
    g = turn(g, 1)
    near, far = compute(ring - 3)
    far_x, far_g, near, beyond_x, beyond_g = tie((swap(xs[-1], 2), swap(gs[-1], 2), near, beyond_x, beyond_g))
    far_xs, far_gs, nears, fars = far_xs + [far_x], far_gs + [far_g], nears + [near], fars + [far]
    backs = [swap(far, 2) for far in fars[1:]]
    near, far = compute(ring - 2)
    near, far, beyond_x, x, backs = tie((near, far, beyond_x, x, backs))
    (beyond,) = pair_rows((beyond_x,), (beyond_g,), owners, experts, weights, (BF16,))
    sums = [None, *(near + back.astype(F32) for near, back in zip(nears[1:] + [near], backs + [swap(far, 2)]))]
    one, carried = turn(sums[1].astype(BF16), -1), sums[2].astype(BF16)
    x, g, first, carried, beyond = tie((x, g, fars[0], carried, beyond))
    (last,) = pair_rows((x,), (g,), owners, experts, weights, (F32,))
    last, one = tie((last, one))

    for s in range(3, ring):
        carried = turn(carried, 1).astype(F32)
        if s < ring - 1:
            carried = (sums[s] + carried).astype(BF16)
    last = (last + swap(beyond, 2).astype(F32) + carried).astype(BF16)
    total = nears[0] + swap(first, 2).astype(F32)
    return total + turn(last, 1).astype(F32) + one.astype(F32)


def expert_rows(rows_in, rows_grad, gate_w, up_w, down_w):
    pre_gate = jnp.dot(rows_in, gate_w, preferred_element_type=F32)
    pre_up = jnp.dot(rows_in, up_w, preferred_element_type=F32)
    back = lax.dot_general(rows_grad, down_w, LAST, preferred_element_type=F32)
    sig = jax.nn.sigmoid(pre_gate)
    d_gate = (back * pre_up * sig * (1.0 + pre_gate * (1.0 - sig))).astype(BF16)
    d_up = (back * pre_gate * sig).astype(BF16)
    term = lax.dot_general(d_gate, gate_w, LAST, preferred_element_type=F32)
    return term + lax.dot_general(d_up, up_w, LAST, preferred_element_type=F32)


def routed(layer_input, out_grad, expert_ids, gates, w_gate, w_up, w_down):
    owners = lax.axis_size("expert")
    rows, width = layer_input.shape
    choose = expert_ids.shape[1]
    capacity = 5 * rows * choose // (4 * owners)
    flat_ids = expert_ids.reshape(-1)
    flat_gates = gates.reshape(-1)
    assigned = flat_ids.shape[0]
    onehot = flat_ids[:, None] == jnp.arange(owners, dtype=jnp.int32)[None, :]
    earlier = jnp.tril(jnp.ones((assigned, assigned), BF16), -1)
    before = jnp.dot(earlier, onehot.astype(BF16), preferred_element_type=F32)
    position = jnp.sum(jnp.where(onehot, before, 0.0), axis=1).astype(jnp.int32)
    slot = flat_ids * capacity + position
    source = jnp.full((owners * capacity,), -1, jnp.int32).at[slot].set(jnp.arange(assigned, dtype=jnp.int32))
    valid = source >= 0
    safe = jnp.maximum(source, 0)
    token = safe // choose
    send_in = jnp.where(valid[:, None], layer_input[token], jnp.zeros((), BF16))
    gate_val = jnp.where(valid, flat_gates[safe], 0.0)
    send_grad = (gate_val[:, None] * out_grad[token].astype(F32)).astype(BF16)

    def exchange(value):
        value = value.reshape(owners, capacity, width)
        value = lax.all_to_all(value, "expert", split_axis=0, concat_axis=0, tiled=True)
        return value.reshape(owners * capacity, width)

    term = expert_rows(exchange(send_in), exchange(send_grad), w_gate[0], w_up[0], w_down[0])
    picked = exchange(term)[slot].reshape(rows, choose, width)
    return jnp.sum(picked, axis=1)


def on_device(layer_input, out_grad, expert_ids, gates, w_gate, w_up, w_down):
    owners = lax.axis_size("expert")
    dense = owners % 4 == 0 and owners >= 16 and expert_ids.shape[1] * 4 >= owners
    plan = gathered if dense else routed
    return plan(layer_input, out_grad, expert_ids, gates, w_gate, w_up, w_down)


def solution(mesh):
    rows = P(("group", "expert"), None)
    owned = P("expert", None, None)
    return jax.shard_map(
        on_device,
        mesh=mesh,
        in_specs=(rows, rows, rows, rows, owned, owned, owned),
        out_specs=rows,
        check_vma=False,
    )
```

```python
from functools import partial

import jax
import jax.numpy as jnp
from jax import lax
from jax.experimental import pallas as pl
from jax.experimental.pallas import tpu as pltpu
from jax.sharding import PartitionSpec as P

F32 = jnp.float32
BF16 = jnp.bfloat16
LAST = (((1,), (1,)), ((), ()))


def gated_kernel(owners, ids, gates, grad, out):
    width = grad.shape[1]
    out[:, :width] = grad[...]
    lane = lax.broadcasted_iota(jnp.int32, (out.shape[1] - width, grad.shape[0]), 0)
    expert = lax.rem(lane, owners)
    high = jnp.zeros(lane.shape, F32)
    for k in range(ids.shape[0]):
        high = jnp.where(ids[k : k + 1, :] == expert, gates[k : k + 1, :], high)
    low = high - high.astype(BF16).astype(F32)
    lowest = low - low.astype(BF16).astype(F32)
    parts = jnp.where(lane < owners, high, jnp.where(lane < 2 * owners, low, lowest))
    parts = jnp.where(lane < 3 * owners, parts, 0.0)
    out[:, width:] = parts.T.astype(BF16)


def gated_rows(grad, ids, gates, owners):
    rows, width = grad.shape
    near = pl.BlockSpec(memory_space=pltpu.VMEM)
    return pl.pallas_call(
        partial(gated_kernel, owners),
        in_specs=[near] * 3,
        out_specs=near,
        out_shape=jax.ShapeDtypeStruct((rows, width + -(-3 * owners // 128) * 128), BF16),
        name="gated_rows",
    )(ids.T, gates.T, grad)


def pair_kernel(pieces, blocks, owners, wide, experts, *refs):
    xs, gs = refs[:pieces], refs[pieces : pieces + blocks]
    refs = refs[pieces + blocks :]
    weights, outs = refs[:6], refs[6 : 6 + blocks]
    x_buf, g_buf, w_in, w_out, d_buf, sems = refs[6 + blocks :]
    rows = gs[0].shape[0]
    width, hidden = weights[0].shape
    copies = {}

    def start(key, source, target):
        copies[key] = pltpu.make_async_copy(source, target, sems.at[len(copies)])
        copies[key].start()

    at = 0
    for i in range(pieces):
        start(("x", i), xs[i], x_buf.at[pl.ds(at, xs[i].shape[0])])
        at = at + xs[i].shape[0]
    start(("w", 0), weights[0], w_in.at[:, pl.ds(0, hidden)])
    start(("w", 1), weights[1], w_in.at[:, pl.ds(hidden, hidden)])
    for i in range(blocks):
        start(("g", i), gs[i], g_buf.at[pl.ds(i * rows, rows)])
    start(("w", 2), weights[2], w_out.at[pl.ds(0, hidden)])
    start(("w", 3), weights[3], w_in.at[:, pl.ds(2 * hidden, hidden)])
    start(("w", 4), weights[4], w_in.at[:, pl.ds(3 * hidden, hidden)])
    start(("w", 5), weights[5], w_out.at[pl.ds(hidden, hidden)])
    for i in range(pieces):
        copies["x", i].wait()
    for k in range(2):
        at = 2 * k * hidden
        copies["w", 3 * k].wait()
        pre_gate = jnp.dot(x_buf[...], w_in[:, at : at + hidden], preferred_element_type=F32)
        copies["w", 3 * k + 1].wait()
        pre_up = jnp.dot(x_buf[...], w_in[:, at + hidden : at + 2 * hidden], preferred_element_type=F32)
        if k == 0:
            for i in range(blocks):
                copies["g", i].wait()
            parts = g_buf[:, width:].astype(F32)
            lane = lax.broadcasted_iota(jnp.int32, parts.shape, 1)
        chosen = (lane == experts[k]) | (lane == experts[k] + owners) | (lane == experts[k] + 2 * owners)
        gate = jnp.sum(jnp.where(chosen, parts, 0.0), axis=1, keepdims=True)
        scaled = (gate * g_buf[:, :width].astype(F32)).astype(BF16)
        copies["w", 3 * k + 2].wait()
        back = lax.dot_general(
            scaled, w_out[k * hidden : (k + 1) * hidden, :], LAST, preferred_element_type=F32
        )
        sig = jax.nn.sigmoid(pre_gate)
        back_sig = back * sig
        d_buf[:, at : at + hidden] = (back_sig * pre_up * (1.0 + pre_gate * (1.0 - sig))).astype(BF16)
        d_buf[:, at + hidden : at + 2 * hidden] = (back_sig * pre_gate).astype(BF16)
    for c in range(0, width, wide):
        term = lax.dot_general(d_buf[...], w_in[c : c + wide, :], LAST, preferred_element_type=F32)
        for i, out in enumerate(outs):
            out[:, c : c + wide] = term[i * rows : (i + 1) * rows, :].astype(out.dtype)


def pair_rows(xs, gs, owners, experts, weights, kinds):
    pieces, blocks = len(xs), len(gs)
    rows, width = gs[0].shape[0], xs[0].shape[1]
    hidden = weights[0].shape[1]
    there = pl.BlockSpec(memory_space=pltpu.HBM)
    near = pl.BlockSpec(memory_space=pltpu.VMEM)
    count = blocks * rows
    return pl.pallas_call(
        partial(pair_kernel, pieces, blocks, owners, 512 if width % 512 == 0 else width),
        in_specs=[pl.BlockSpec(memory_space=pltpu.SMEM)] + [there] * (pieces + blocks) + [pl.BlockSpec(memory_space=pl.ANY)] * 6,
        out_specs=[near] * blocks,
        out_shape=[jax.ShapeDtypeStruct((rows, width), kind) for kind in kinds],
        scratch_shapes=[
            pltpu.VMEM((count, width), BF16),
            pltpu.VMEM((count, gs[0].shape[1]), BF16),
            pltpu.VMEM((width, 4 * hidden), BF16),
            pltpu.VMEM((2 * hidden, width), BF16),
            pltpu.VMEM((count, 4 * hidden), BF16),
            pltpu.SemaphoreType.DMA((pieces + blocks + 6,)),
        ],
        compiler_params=pltpu.CompilerParams(vmem_limit_bytes=36 * 2**20),
        cost_estimate=pl.CostEstimate(
            flops=20 * count * width * hidden,
            bytes_accessed=12 * width * hidden + 7 * count * width,
            transcendentals=2 * count * hidden,
        ),
        name="pair_rows",
    )(experts, *xs, *gs, *weights)


def gathered(layer_input, out_grad, expert_ids, gates, w_gate, w_up, w_down):
    owners = lax.axis_size("expert")
    ring = owners // 4
    me = lax.axis_index("expert")
    experts = jnp.stack([me, me ^ 1]).astype(jnp.int32)

    def turn(value, by):
        return lax.ppermute(value, "expert", [(i, (i + 4 * by) % owners) for i in range(owners)])

    def swap(value, bit):
        return lax.ppermute(value, "expert", [(i, i ^ bit) for i in range(owners)])

    tie = lax.optimization_barrier

    own = (w_gate[0], w_up[0], w_down[0])

    xs, gs = [layer_input], [gated_rows(out_grad, expert_ids, gates, owners)]
    far_xs, far_gs, nears, fars = [], [], [], []

    def compute(s):
        return pair_rows(
            (xs[s], far_xs[s]), (gs[s], far_gs[s]), owners, experts, weights, (F32, BF16)
        )

    for s in range(ring - 2):
        far_x, x, far_g, g = swap(xs[s], 2), turn(xs[s], 1), swap(gs[s], 2), turn(gs[s], 1)
        if s == 0:
            theirs, sent = [swap(own[0], 1)], own[1:]
            far_x, x, far_g, g, theirs, sent = tie((far_x, x, far_g, g, theirs, sent))
            weights = (*own, *theirs, *(swap(w, 1) for w in sent))
        else:
            near, far = compute(s - 1)
            far_x, x = tie((far_x, x))
            far_g, g, near = tie((far_g, g, near))
            nears.append(near)
            fars.append(far)
        xs, gs, far_xs, far_gs = xs + [x], gs + [g], far_xs + [far_x], far_gs + [far_g]

    half = xs[0].shape[0] // 2
    x_last, beyond_g = turn(xs[0], -1), turn(far_gs[0], -1)
    far_x, x_last = tie((far_xs[0], x_last))
    top, bottom = turn(far_x[:half], -1), swap(x_last[half:], 2)
    g_last, beyond_g = tie((gs[0], beyond_g))
    g_last = turn(g_last, -1)
    near, far = compute(ring - 3)
    far_x, far_g, near, beyond_g = tie((swap(xs[-1], 2), swap(gs[-1], 2), near, beyond_g))
    far_xs, far_gs, nears, fars = far_xs + [far_x], far_gs + [far_g], nears + [near], fars + [far]
    backs = [swap(far, 2) for far in fars[1:]]
    near, far = compute(ring - 2)
    near, far, top, bottom, backs = tie((near, far, top, bottom, backs))
    (beyond,) = pair_rows((top, bottom), (beyond_g,), owners, experts, weights, (BF16,))
    sums = [None, *(near + back.astype(F32) for near, back in zip(nears[1:] + [near], backs + [swap(far, 2)]))]
    one, carried = turn(sums[1].astype(BF16), -1), sums[2].astype(BF16)
    x, g, first, carried, beyond = tie((x_last, g_last, fars[0], carried, beyond))
    (last,) = pair_rows((x,), (g,), owners, experts, weights, (F32,))
    last, one = tie((last, one))

    for s in range(3, ring):
        carried = turn(carried, 1).astype(F32)
        if s < ring - 1:
            carried = (sums[s] + carried).astype(BF16)
    last = (last + swap(beyond, 2).astype(F32) + carried).astype(BF16)
    total = nears[0] + swap(first, 2).astype(F32)
    return total + turn(last, 1).astype(F32) + one.astype(F32)


def expert_rows(rows_in, rows_grad, gate_w, up_w, down_w):
    pre_gate = jnp.dot(rows_in, gate_w, preferred_element_type=F32)
    pre_up = jnp.dot(rows_in, up_w, preferred_element_type=F32)
    back = lax.dot_general(rows_grad, down_w, LAST, preferred_element_type=F32)
    sig = jax.nn.sigmoid(pre_gate)
    d_gate = (back * pre_up * sig * (1.0 + pre_gate * (1.0 - sig))).astype(BF16)
    d_up = (back * pre_gate * sig).astype(BF16)
    term = lax.dot_general(d_gate, gate_w, LAST, preferred_element_type=F32)
    return term + lax.dot_general(d_up, up_w, LAST, preferred_element_type=F32)


def routed(layer_input, out_grad, expert_ids, gates, w_gate, w_up, w_down):
    owners = lax.axis_size("expert")
    rows, width = layer_input.shape
    choose = expert_ids.shape[1]
    capacity = 5 * rows * choose // (4 * owners)
    flat_ids = expert_ids.reshape(-1)
    flat_gates = gates.reshape(-1)
    assigned = flat_ids.shape[0]
    onehot = flat_ids[:, None] == jnp.arange(owners, dtype=jnp.int32)[None, :]
    earlier = jnp.tril(jnp.ones((assigned, assigned), BF16), -1)
    before = jnp.dot(earlier, onehot.astype(BF16), preferred_element_type=F32)
    position = jnp.sum(jnp.where(onehot, before, 0.0), axis=1).astype(jnp.int32)
    slot = flat_ids * capacity + position
    source = jnp.full((owners * capacity,), -1, jnp.int32).at[slot].set(jnp.arange(assigned, dtype=jnp.int32))
    valid = source >= 0
    safe = jnp.maximum(source, 0)
    token = safe // choose
    send_in = jnp.where(valid[:, None], layer_input[token], jnp.zeros((), BF16))
    gate_val = jnp.where(valid, flat_gates[safe], 0.0)
    send_grad = (gate_val[:, None] * out_grad[token].astype(F32)).astype(BF16)

    def exchange(value):
        value = value.reshape(owners, capacity, width)
        value = lax.all_to_all(value, "expert", split_axis=0, concat_axis=0, tiled=True)
        return value.reshape(owners * capacity, width)

    term = expert_rows(exchange(send_in), exchange(send_grad), w_gate[0], w_up[0], w_down[0])
    picked = exchange(term)[slot].reshape(rows, choose, width)
    return jnp.sum(picked, axis=1)


def on_device(layer_input, out_grad, expert_ids, gates, w_gate, w_up, w_down):
    owners = lax.axis_size("expert")
    dense = owners % 4 == 0 and owners >= 16 and expert_ids.shape[1] * 4 >= owners
    plan = gathered if dense else routed
    return plan(layer_input, out_grad, expert_ids, gates, w_gate, w_up, w_down)


def solution(mesh):
    rows = P(("group", "expert"), None)
    owned = P("expert", None, None)
    return jax.shard_map(
        on_device,
        mesh=mesh,
        in_specs=(rows, rows, rows, rows, owned, owned, owned),
        out_specs=rows,
        check_vma=False,
    )
```

```python
from functools import partial

import jax
import jax.numpy as jnp
from jax import lax
from jax.experimental import pallas as pl
from jax.experimental.pallas import tpu as pltpu
from jax.sharding import PartitionSpec as P

F32 = jnp.float32
BF16 = jnp.bfloat16
LAST = (((1,), (1,)), ((), ()))


def gated_kernel(owners, ids, gates, grad, out):
    width = grad.shape[1]
    out[:, :width] = grad[...]
    lane = lax.broadcasted_iota(jnp.int32, (out.shape[1] - width, grad.shape[0]), 0)
    expert = lax.rem(lane, owners)
    high = jnp.zeros(lane.shape, F32)
    for k in range(ids.shape[0]):
        high = jnp.where(ids[k : k + 1, :] == expert, gates[k : k + 1, :], high)
    low = high - high.astype(BF16).astype(F32)
    lowest = low - low.astype(BF16).astype(F32)
    parts = jnp.where(lane < owners, high, jnp.where(lane < 2 * owners, low, lowest))
    parts = jnp.where(lane < 3 * owners, parts, 0.0)
    out[:, width:] = parts.T.astype(BF16)


def gated_rows(grad, ids, gates, owners):
    rows, width = grad.shape
    near = pl.BlockSpec(memory_space=pltpu.VMEM)
    return pl.pallas_call(
        partial(gated_kernel, owners),
        in_specs=[near] * 3,
        out_specs=near,
        out_shape=jax.ShapeDtypeStruct((rows, width + -(-3 * owners // 128) * 128), BF16),
        name="gated_rows",
    )(ids.T, gates.T, grad)


def pair_kernel(pieces, blocks, owners, wide, experts, *refs):
    xs, gs = refs[:pieces], refs[pieces : pieces + blocks]
    refs = refs[pieces + blocks :]
    weights, outs = refs[:6], refs[6 : 6 + blocks]
    x_buf, g_buf, w_in, w_out, d_buf, sems = refs[6 + blocks :]
    rows = gs[0].shape[0]
    width, hidden = weights[0].shape
    copies = {}

    def start(key, source, target):
        copies[key] = pltpu.make_async_copy(source, target, sems.at[len(copies)])
        copies[key].start()

    at = 0
    for i in range(pieces):
        start(("x", i), xs[i], x_buf.at[pl.ds(at, xs[i].shape[0])])
        at = at + xs[i].shape[0]
    start(("w", 0), weights[0], w_in.at[:, pl.ds(0, hidden)])
    start(("w", 1), weights[1], w_in.at[:, pl.ds(hidden, hidden)])
    for i in range(blocks):
        start(("g", i), gs[i], g_buf.at[pl.ds(i * rows, rows)])
    start(("w", 2), weights[2], w_out.at[pl.ds(0, hidden)])
    start(("w", 3), weights[3], w_in.at[:, pl.ds(2 * hidden, hidden)])
    start(("w", 4), weights[4], w_in.at[:, pl.ds(3 * hidden, hidden)])
    start(("w", 5), weights[5], w_out.at[pl.ds(hidden, hidden)])
    for i in range(pieces):
        copies["x", i].wait()
    for k in range(2):
        at = 2 * k * hidden
        copies["w", 3 * k].wait()
        pre_gate = jnp.dot(x_buf[...], w_in[:, at : at + hidden], preferred_element_type=F32)
        copies["w", 3 * k + 1].wait()
        pre_up = jnp.dot(x_buf[...], w_in[:, at + hidden : at + 2 * hidden], preferred_element_type=F32)
        if k == 0:
            for i in range(blocks):
                copies["g", i].wait()
            parts = g_buf[:, width:].astype(F32)
            lane = lax.broadcasted_iota(jnp.int32, parts.shape, 1)
        chosen = (lane == experts[k]) | (lane == experts[k] + owners) | (lane == experts[k] + 2 * owners)
        gate = jnp.sum(jnp.where(chosen, parts, 0.0), axis=1, keepdims=True)
        scaled = (gate * g_buf[:, :width].astype(F32)).astype(BF16)
        copies["w", 3 * k + 2].wait()
        back = lax.dot_general(
            scaled, w_out[k * hidden : (k + 1) * hidden, :], LAST, preferred_element_type=F32
        )
        sig = jax.nn.sigmoid(pre_gate)
        back_sig = back * sig
        d_buf[:, at : at + hidden] = (back_sig * pre_up * (1.0 + pre_gate * (1.0 - sig))).astype(BF16)
        d_buf[:, at + hidden : at + 2 * hidden] = (back_sig * pre_gate).astype(BF16)
    for c in range(0, width, wide):
        term = lax.dot_general(d_buf[...], w_in[c : c + wide, :], LAST, preferred_element_type=F32)
        for i, out in enumerate(outs):
            out[:, c : c + wide] = term[i * rows : (i + 1) * rows, :].astype(out.dtype)


def pair_rows(xs, gs, owners, experts, weights, kinds):
    pieces, blocks = len(xs), len(gs)
    rows, width = gs[0].shape[0], xs[0].shape[1]
    hidden = weights[0].shape[1]
    there = pl.BlockSpec(memory_space=pltpu.HBM)
    near = pl.BlockSpec(memory_space=pltpu.VMEM)
    count = blocks * rows
    return pl.pallas_call(
        partial(pair_kernel, pieces, blocks, owners, 512 if width % 512 == 0 else width),
        in_specs=[pl.BlockSpec(memory_space=pltpu.SMEM)] + [there] * (pieces + blocks) + [pl.BlockSpec(memory_space=pl.ANY)] * 6,
        out_specs=[near] * blocks,
        out_shape=[jax.ShapeDtypeStruct((rows, width), kind) for kind in kinds],
        scratch_shapes=[
            pltpu.VMEM((count, width), BF16),
            pltpu.VMEM((count, gs[0].shape[1]), BF16),
            pltpu.VMEM((width, 4 * hidden), BF16),
            pltpu.VMEM((2 * hidden, width), BF16),
            pltpu.VMEM((count, 4 * hidden), BF16),
            pltpu.SemaphoreType.DMA((pieces + blocks + 6,)),
        ],
        compiler_params=pltpu.CompilerParams(vmem_limit_bytes=36 * 2**20),
        cost_estimate=pl.CostEstimate(
            flops=20 * count * width * hidden,
            bytes_accessed=12 * width * hidden + 7 * count * width,
            transcendentals=2 * count * hidden,
        ),
        name="pair_rows",
    )(experts, *xs, *gs, *weights)


def gathered(layer_input, out_grad, expert_ids, gates, w_gate, w_up, w_down):
    owners = lax.axis_size("expert")
    ring = owners // 4
    me = lax.axis_index("expert")
    experts = jnp.stack([me, me ^ 1]).astype(jnp.int32)

    def turn(value, by):
        return lax.ppermute(value, "expert", [(i, (i + 4 * by) % owners) for i in range(owners)])

    def swap(value, bit):
        return lax.ppermute(value, "expert", [(i, i ^ bit) for i in range(owners)])

    tie = lax.optimization_barrier

    own = (w_gate[0], w_up[0], w_down[0])

    xs, gs = [layer_input], [gated_rows(out_grad, expert_ids, gates, owners)]
    far_xs, far_gs, nears, fars = [], [], [], []

    def compute(s):
        return pair_rows(
            (xs[s], far_xs[s]), (gs[s], far_gs[s]), owners, experts, weights, (F32, BF16)
        )

    for s in range(ring - 2):
        far_x, x, far_g, g = swap(xs[s], 2), turn(xs[s], 1), swap(gs[s], 2), turn(gs[s], 1)
        if s == 0:
            theirs, sent = [swap(own[0], 1)], own[1:]
            far_x, x, far_g, g, theirs, sent = tie((far_x, x, far_g, g, theirs, sent))
            weights = (*own, *theirs, *(swap(w, 1) for w in sent))
        else:
            near, far = compute(s - 1)
            far_x, x = tie((far_x, x))
            far_g, g, near = tie((far_g, g, near))
            nears.append(near)
            fars.append(far)
        xs, gs, far_xs, far_gs = xs + [x], gs + [g], far_xs + [far_x], far_gs + [far_g]

    half = xs[0].shape[0] // 2
    x_last, beyond_g = turn(xs[0], -1), turn(far_gs[0], -1)
    far_x, x_last = tie((far_xs[0], x_last))
    top, bottom = turn(far_x[:half], -1), swap(x_last[half:], 2)
    g_last, beyond_g = tie((gs[0], beyond_g))
    g_last = turn(g_last, -1)
    near, far = compute(ring - 3)
    far_x, far_g, near, beyond_g = tie((swap(xs[-1], 2), swap(gs[-1], 2), near, beyond_g))
    far_xs, far_gs, nears, fars = far_xs + [far_x], far_gs + [far_g], nears + [near], fars + [far]
    backs = [swap(far, 2) for far in fars[1:]]
    near, far = compute(ring - 2)
    near, far, top, bottom, backs, g_last = tie((near, far, top, bottom, backs, g_last))
    (beyond,) = pair_rows((top, bottom), (beyond_g,), owners, experts, weights, (BF16,))
    sums = [None, *(near + back.astype(F32) for near, back in zip(nears[1:] + [near], backs + [swap(far, 2)]))]
    one, carried = turn(sums[1].astype(BF16), -1), sums[2].astype(BF16)
    x, g, first, carried, beyond = tie((x_last, g_last, fars[0], carried, beyond))
    (last,) = pair_rows((x,), (g,), owners, experts, weights, (F32,))
    last, one = tie((last, one))

    for s in range(3, ring):
        carried = turn(carried, 1).astype(F32)
        if s < ring - 1:
            carried = (sums[s] + carried).astype(BF16)
    last = (last + swap(beyond, 2).astype(F32) + carried).astype(BF16)
    total = nears[0] + swap(first, 2).astype(F32)
    return total + turn(last, 1).astype(F32) + one.astype(F32)


def expert_rows(rows_in, rows_grad, gate_w, up_w, down_w):
    pre_gate = jnp.dot(rows_in, gate_w, preferred_element_type=F32)
    pre_up = jnp.dot(rows_in, up_w, preferred_element_type=F32)
    back = lax.dot_general(rows_grad, down_w, LAST, preferred_element_type=F32)
    sig = jax.nn.sigmoid(pre_gate)
    d_gate = (back * pre_up * sig * (1.0 + pre_gate * (1.0 - sig))).astype(BF16)
    d_up = (back * pre_gate * sig).astype(BF16)
    term = lax.dot_general(d_gate, gate_w, LAST, preferred_element_type=F32)
    return term + lax.dot_general(d_up, up_w, LAST, preferred_element_type=F32)


def routed(layer_input, out_grad, expert_ids, gates, w_gate, w_up, w_down):
    owners = lax.axis_size("expert")
    rows, width = layer_input.shape
    choose = expert_ids.shape[1]
    capacity = 5 * rows * choose // (4 * owners)
    flat_ids = expert_ids.reshape(-1)
    flat_gates = gates.reshape(-1)
    assigned = flat_ids.shape[0]
    onehot = flat_ids[:, None] == jnp.arange(owners, dtype=jnp.int32)[None, :]
    earlier = jnp.tril(jnp.ones((assigned, assigned), BF16), -1)
    before = jnp.dot(earlier, onehot.astype(BF16), preferred_element_type=F32)
    position = jnp.sum(jnp.where(onehot, before, 0.0), axis=1).astype(jnp.int32)
    slot = flat_ids * capacity + position
    source = jnp.full((owners * capacity,), -1, jnp.int32).at[slot].set(jnp.arange(assigned, dtype=jnp.int32))
    valid = source >= 0
    safe = jnp.maximum(source, 0)
    token = safe // choose
    send_in = jnp.where(valid[:, None], layer_input[token], jnp.zeros((), BF16))
    gate_val = jnp.where(valid, flat_gates[safe], 0.0)
    send_grad = (gate_val[:, None] * out_grad[token].astype(F32)).astype(BF16)

    def exchange(value):
        value = value.reshape(owners, capacity, width)
        value = lax.all_to_all(value, "expert", split_axis=0, concat_axis=0, tiled=True)
        return value.reshape(owners * capacity, width)

    term = expert_rows(exchange(send_in), exchange(send_grad), w_gate[0], w_up[0], w_down[0])
    picked = exchange(term)[slot].reshape(rows, choose, width)
    return jnp.sum(picked, axis=1)


def on_device(layer_input, out_grad, expert_ids, gates, w_gate, w_up, w_down):
    owners = lax.axis_size("expert")
    dense = owners % 4 == 0 and owners >= 16 and expert_ids.shape[1] * 4 >= owners
    plan = gathered if dense else routed
    return plan(layer_input, out_grad, expert_ids, gates, w_gate, w_up, w_down)


def solution(mesh):
    rows = P(("group", "expert"), None)
    owned = P("expert", None, None)
    return jax.shard_map(
        on_device,
        mesh=mesh,
        in_specs=(rows, rows, rows, rows, owned, owned, owned),
        out_specs=rows,
        check_vma=False,
    )
```

```python
from functools import partial

import jax
import jax.numpy as jnp
from jax import lax
from jax.experimental import pallas as pl
from jax.experimental.pallas import tpu as pltpu
from jax.sharding import PartitionSpec as P

F32 = jnp.float32
BF16 = jnp.bfloat16
LAST = (((1,), (1,)), ((), ()))


def gated_kernel(owners, ids, gates, grad, out):
    width = grad.shape[1]
    out[:, :width] = grad[...]
    lane = lax.broadcasted_iota(jnp.int32, (out.shape[1] - width, grad.shape[0]), 0)
    expert = lax.rem(lane, owners)
    high = jnp.zeros(lane.shape, F32)
    for k in range(ids.shape[0]):
        high = jnp.where(ids[k : k + 1, :] == expert, gates[k : k + 1, :], high)
    low = high - high.astype(BF16).astype(F32)
    lowest = low - low.astype(BF16).astype(F32)
    parts = jnp.where(lane < owners, high, jnp.where(lane < 2 * owners, low, lowest))
    parts = jnp.where(lane < 3 * owners, parts, 0.0)
    out[:, width:] = parts.T.astype(BF16)


def gated_rows(grad, ids, gates, owners):
    rows, width = grad.shape
    near = pl.BlockSpec(memory_space=pltpu.VMEM)
    return pl.pallas_call(
        partial(gated_kernel, owners),
        in_specs=[near] * 3,
        out_specs=near,
        out_shape=jax.ShapeDtypeStruct((rows, width + -(-3 * owners // 128) * 128), BF16),
        name="gated_rows",
    )(ids.T, gates.T, grad)


def pair_kernel(pieces, blocks, owners, wide, experts, *refs):
    xs, gs = refs[:pieces], refs[pieces : pieces + blocks]
    refs = refs[pieces + blocks :]
    weights, outs = refs[:6], refs[6 : 6 + blocks]
    x_buf, g_buf, w_in, w_out, d_buf, sems = refs[6 + blocks :]
    rows = gs[0].shape[0]
    width, hidden = weights[0].shape
    copies = {}

    def start(key, source, target):
        copies[key] = pltpu.make_async_copy(source, target, sems.at[len(copies)])
        copies[key].start()

    at = 0
    for i in range(pieces):
        start(("x", i), xs[i], x_buf.at[pl.ds(at, xs[i].shape[0])])
        at = at + xs[i].shape[0]
    start(("w", 0), weights[0], w_in.at[:, pl.ds(0, hidden)])
    start(("w", 1), weights[1], w_in.at[:, pl.ds(hidden, hidden)])
    for i in range(blocks):
        start(("g", i), gs[i], g_buf.at[pl.ds(i * rows, rows)])
    start(("w", 2), weights[2], w_out.at[pl.ds(0, hidden)])
    start(("w", 3), weights[3], w_in.at[:, pl.ds(2 * hidden, hidden)])
    start(("w", 4), weights[4], w_in.at[:, pl.ds(3 * hidden, hidden)])
    start(("w", 5), weights[5], w_out.at[pl.ds(hidden, hidden)])
    for i in range(pieces):
        copies["x", i].wait()
    for k in range(2):
        at = 2 * k * hidden
        copies["w", 3 * k].wait()
        pre_gate = jnp.dot(x_buf[...], w_in[:, at : at + hidden], preferred_element_type=F32)
        copies["w", 3 * k + 1].wait()
        pre_up = jnp.dot(x_buf[...], w_in[:, at + hidden : at + 2 * hidden], preferred_element_type=F32)
        if k == 0:
            for i in range(blocks):
                copies["g", i].wait()
            parts = g_buf[:, width:].astype(F32)
            lane = lax.broadcasted_iota(jnp.int32, parts.shape, 1)
        chosen = (lane == experts[k]) | (lane == experts[k] + owners) | (lane == experts[k] + 2 * owners)
        gate = jnp.sum(jnp.where(chosen, parts, 0.0), axis=1, keepdims=True)
        scaled = (gate * g_buf[:, :width].astype(F32)).astype(BF16)
        copies["w", 3 * k + 2].wait()
        back = lax.dot_general(
            scaled, w_out[k * hidden : (k + 1) * hidden, :], LAST, preferred_element_type=F32
        )
        sig = jax.nn.sigmoid(pre_gate)
        back_sig = back * sig
        d_buf[:, at : at + hidden] = (back_sig * pre_up * (1.0 + pre_gate * (1.0 - sig))).astype(BF16)
        d_buf[:, at + hidden : at + 2 * hidden] = (back_sig * pre_gate).astype(BF16)
    for c in range(0, width, wide):
        term = lax.dot_general(d_buf[...], w_in[c : c + wide, :], LAST, preferred_element_type=F32)
        for i, out in enumerate(outs):
            out[:, c : c + wide] = term[i * rows : (i + 1) * rows, :].astype(out.dtype)


def pair_rows(xs, gs, owners, experts, weights, kinds):
    pieces, blocks = len(xs), len(gs)
    rows, width = gs[0].shape[0], xs[0].shape[1]
    hidden = weights[0].shape[1]
    there = pl.BlockSpec(memory_space=pltpu.HBM)
    near = pl.BlockSpec(memory_space=pltpu.VMEM)
    count = blocks * rows
    return pl.pallas_call(
        partial(pair_kernel, pieces, blocks, owners, 512 if width % 512 == 0 else width),
        in_specs=[pl.BlockSpec(memory_space=pltpu.SMEM)] + [there] * (pieces + blocks) + [pl.BlockSpec(memory_space=pl.ANY)] * 6,
        out_specs=[near] * blocks,
        out_shape=[jax.ShapeDtypeStruct((rows, width), kind) for kind in kinds],
        scratch_shapes=[
            pltpu.VMEM((count, width), BF16),
            pltpu.VMEM((count, gs[0].shape[1]), BF16),
            pltpu.VMEM((width, 4 * hidden), BF16),
            pltpu.VMEM((2 * hidden, width), BF16),
            pltpu.VMEM((count, 4 * hidden), BF16),
            pltpu.SemaphoreType.DMA((pieces + blocks + 6,)),
        ],
        compiler_params=pltpu.CompilerParams(vmem_limit_bytes=36 * 2**20),
        cost_estimate=pl.CostEstimate(
            flops=20 * count * width * hidden,
            bytes_accessed=12 * width * hidden + 7 * count * width,
            transcendentals=2 * count * hidden,
        ),
        name="pair_rows",
    )(experts, *xs, *gs, *weights)


def gathered(layer_input, out_grad, expert_ids, gates, w_gate, w_up, w_down):
    owners = lax.axis_size("expert")
    ring = owners // 4
    me = lax.axis_index("expert")
    experts = jnp.stack([me, me ^ 1]).astype(jnp.int32)

    def turn(value, by):
        return lax.ppermute(value, "expert", [(i, (i + 4 * by) % owners) for i in range(owners)])

    def swap(value, bit):
        return lax.ppermute(value, "expert", [(i, i ^ bit) for i in range(owners)])

    tie = lax.optimization_barrier

    own = (w_gate[0], w_up[0], w_down[0])

    xs, gs = [layer_input], [gated_rows(out_grad, expert_ids, gates, owners)]
    far_xs, far_gs, nears, fars = [], [], [], []

    def compute(s):
        return pair_rows(
            (xs[s], far_xs[s]), (gs[s], far_gs[s]), owners, experts, weights, (F32, BF16)
        )

    for s in range(ring - 2):
        far_x, x, far_g, g = swap(xs[s], 2), turn(xs[s], 1), swap(gs[s], 2), turn(gs[s], 1)
        if s == 0:
            theirs, sent = [swap(own[0], 1)], own[1:]
            far_x, x, far_g, g, theirs, sent = tie((far_x, x, far_g, g, theirs, sent))
            weights = (*own, *theirs, *(swap(w, 1) for w in sent))
        else:
            near, far = compute(s - 1)
            far_x, x = tie((far_x, x))
            far_g, g, near = tie((far_g, g, near))
            nears.append(near)
            fars.append(far)
        xs, gs, far_xs, far_gs = xs + [x], gs + [g], far_xs + [far_x], far_gs + [far_g]

    half = xs[0].shape[0] // 2
    x_last, beyond_g = turn(xs[0], -1), turn(far_gs[0], -1)
    far_x, x_last = tie((far_xs[0], x_last))
    top, bottom = turn(far_x[:half], -1), swap(x_last[half:], 2)
    g_last, beyond_g = tie((gs[0], beyond_g))
    g_last = turn(g_last, -1)
    near, far = compute(ring - 3)
    far_x, far_g, near, beyond_g = tie((swap(xs[-1], 2), swap(gs[-1], 2), near, beyond_g))
    far_xs, far_gs, nears, fars = far_xs + [far_x], far_gs + [far_g], nears + [near], fars + [far]
    backs = [swap(far, 2) for far in fars[1:]]
    near, far = compute(ring - 2)
    near, far, top, bottom, backs, g_last = tie((near, far, top, bottom, backs, g_last))
    (beyond,) = pair_rows((top, bottom), (beyond_g,), owners, experts, weights, (BF16,))
    sums = [None, *(near + back.astype(F32) for near, back in zip(nears[1:] + [near], backs + [swap(far, 2)]))]
    one, carried = turn(sums[1].astype(BF16), -1), sums[2].astype(BF16)
    x, g, first, carried, beyond = tie((x_last, g_last, fars[0], carried, beyond))
    (last,) = pair_rows((x,), (g,), owners, experts, weights, (F32,))
    last, one = tie((last, one))

    for s in range(3, ring):
        carried = turn(carried, 1).astype(F32)
        if s < ring - 1:
            carried = (sums[s] + carried).astype(BF16)
    last = (last + swap(beyond, 2).astype(F32) + carried).astype(BF16)
    total = nears[0] + swap(first, 2).astype(F32) + one.astype(F32)
    total, last = tie((total, turn(last, 1)))
    return total + last.astype(F32)


def expert_rows(rows_in, rows_grad, gate_w, up_w, down_w):
    pre_gate = jnp.dot(rows_in, gate_w, preferred_element_type=F32)
    pre_up = jnp.dot(rows_in, up_w, preferred_element_type=F32)
    back = lax.dot_general(rows_grad, down_w, LAST, preferred_element_type=F32)
    sig = jax.nn.sigmoid(pre_gate)
    d_gate = (back * pre_up * sig * (1.0 + pre_gate * (1.0 - sig))).astype(BF16)
    d_up = (back * pre_gate * sig).astype(BF16)
    term = lax.dot_general(d_gate, gate_w, LAST, preferred_element_type=F32)
    return term + lax.dot_general(d_up, up_w, LAST, preferred_element_type=F32)


def routed(layer_input, out_grad, expert_ids, gates, w_gate, w_up, w_down):
    owners = lax.axis_size("expert")
    rows, width = layer_input.shape
    choose = expert_ids.shape[1]
    capacity = 5 * rows * choose // (4 * owners)
    flat_ids = expert_ids.reshape(-1)
    flat_gates = gates.reshape(-1)
    assigned = flat_ids.shape[0]
    onehot = flat_ids[:, None] == jnp.arange(owners, dtype=jnp.int32)[None, :]
    earlier = jnp.tril(jnp.ones((assigned, assigned), BF16), -1)
    before = jnp.dot(earlier, onehot.astype(BF16), preferred_element_type=F32)
    position = jnp.sum(jnp.where(onehot, before, 0.0), axis=1).astype(jnp.int32)
    slot = flat_ids * capacity + position
    source = jnp.full((owners * capacity,), -1, jnp.int32).at[slot].set(jnp.arange(assigned, dtype=jnp.int32))
    valid = source >= 0
    safe = jnp.maximum(source, 0)
    token = safe // choose
    send_in = jnp.where(valid[:, None], layer_input[token], jnp.zeros((), BF16))
    gate_val = jnp.where(valid, flat_gates[safe], 0.0)
    send_grad = (gate_val[:, None] * out_grad[token].astype(F32)).astype(BF16)

    def exchange(value):
        value = value.reshape(owners, capacity, width)
        value = lax.all_to_all(value, "expert", split_axis=0, concat_axis=0, tiled=True)
        return value.reshape(owners * capacity, width)

    term = expert_rows(exchange(send_in), exchange(send_grad), w_gate[0], w_up[0], w_down[0])
    picked = exchange(term)[slot].reshape(rows, choose, width)
    return jnp.sum(picked, axis=1)


def on_device(layer_input, out_grad, expert_ids, gates, w_gate, w_up, w_down):
    owners = lax.axis_size("expert")
    dense = owners % 4 == 0 and owners >= 16 and expert_ids.shape[1] * 4 >= owners
    plan = gathered if dense else routed
    return plan(layer_input, out_grad, expert_ids, gates, w_gate, w_up, w_down)


def solution(mesh):
    rows = P(("group", "expert"), None)
    owned = P("expert", None, None)
    return jax.shard_map(
        on_device,
        mesh=mesh,
        in_specs=(rows, rows, rows, rows, owned, owned, owned),
        out_specs=rows,
        check_vma=False,
    )
```
